256 devices in a mesh: freq: 32 (over z_hi, x, core), beam: 8 (over y, z_lo).
Axes of the slice: x: 4, y: 4, z: 8 (z_hi: 4, z_lo: 2; z = z_hi * 2 + z_lo), core: 2. Of those that a mesh axis runs over, the one named last changes fastest.
Arguments:
- voltages: bfloat16 [2, 16, 1024, 16, 256], P(None, 'beam', 'freq'), parts along dimension 1, may hold values from -6 to 6
- sub_delays: int32 [8192, 512], P('freq'), may hold values from 0 to 31, as said below
- merge_tables: int32 [5, 3, 8192], P(None, None, 'freq'), may hold values from 0 to 255, as said below
Outputs:
- peak_values: float32 [16, 8, 8192], P('beam', None, 'freq'), parts along dimension 0
The draws below stay inside these ranges and needn't reach their ends.
There are 8 independent parts, one for each index of `beam`. The reference program is written for one: setup_inputs(seed, part) draws one part's arguments, and reference() takes and returns one part's arrays. A program takes and returns all parts, laid end to end along the dimension named above; an argument that names none is the same for every part. Nothing has to cross between parts.
Inputs may be any that keep to these rules, and one draw needn't show every extreme that they name: `sub_delays`: every row has some channel with delay 32 - 1. `merge_tables`: for each level and each aligned block of 256 trials, rows 0 and 1 each hold a permutation of 0 to 255; row 2 holds delays of 0 to 63, and each such block has a delay of 63.
All inputs are finite; a program needn't handle non-finite values.
Results may differ from the reference program's by a relative error of at most 0.0003.
Values may be sent and summed in bfloat16 or wider, within the bound.
No kernel may reach another device: no remote copies, remote signals or barrier semaphores. Data moves between devices by JAX's collectives and lax.ppermute only.
A program may use at most 128 MiB of HBM per device.

```python
import math
import jax
import jax.numpy as jnp
from jax import lax

COARSE = 1024
UPCHAN = 16
TAPS = 4
WIDTHS = 8
BEAMS = 2
NT = 256
DM_DEV = 256
SHIFTS = 32
LEVELS = 5
CROSS_SHIFT = 64
N_FREQ = 32


def draw_sub_delays(key, part):
    row_count = DM_DEV * N_FREQ
    col_count = COARSE * UPCHAN // N_FREQ
    first_key, second_key = jax.random.split(jax.random.fold_in(key, 11))
    base = jax.random.randint(first_key, (row_count, col_count), 0, SHIFTS)
    picked = jax.random.randint(second_key, (row_count, 1), 0, col_count)
    columns = jnp.arange(col_count)[None, :]
    return jnp.where(columns == picked, SHIFTS - 1, base).astype(jnp.int32)


def draw_merge_tables(key, part):
    blocks = LEVELS * N_FREQ
    keys = jax.random.split(jax.random.fold_in(key, 23), 2 * blocks + 2)
    permute = jax.vmap(lambda single: jax.random.permutation(single, DM_DEV))
    lower_rows = permute(keys[:blocks]).reshape(LEVELS, N_FREQ * DM_DEV)
    upper_rows = permute(keys[blocks:2 * blocks]).reshape(LEVELS, N_FREQ * DM_DEV)
    delays = jax.random.randint(keys[2 * blocks], (LEVELS, N_FREQ, DM_DEV), 0, CROSS_SHIFT)
    picked = jax.random.randint(keys[2 * blocks + 1], (LEVELS, N_FREQ, 1), 0, DM_DEV)
    delays = jnp.where(jnp.arange(DM_DEV)[None, None, :] == picked, CROSS_SHIFT - 1, delays)
    delays = delays.reshape(LEVELS, N_FREQ * DM_DEV)
    return jnp.stack([lower_rows, upper_rows, delays], axis=1).astype(jnp.int32)


def block_scale(stream_key, dims, pieces, smallest, largest):
    level, own = 1.0, jax.random.fold_in(stream_key, 6)
    for dim, blocks in pieces:
        heights = jnp.exp(jax.random.uniform(jax.random.fold_in(own, dim), (blocks,), jnp.float32, smallest / len(pieces), largest / len(pieces)))
        level = level * jnp.repeat(heights, dims[dim] // blocks).reshape([-1 if axis == dim else 1 for axis in range(len(dims))])
    return level


def noise(own_key, extent, scale, bound, cuts=(), kind=jnp.bfloat16):
    gain = block_scale(own_key, extent, cuts, -0.22, 0.18) if cuts else 1.0
    result = jax.random.normal(own_key, extent, jnp.float32) * scale * gain
    return jnp.minimum(jnp.maximum(result, -bound), bound).astype(kind)


def setup_inputs(seed: int = 0, part: int = 0) -> dict:
    arg_keys = jax.random.split(jax.random.key(seed), 4)
    part_splits = jax.random.split(jax.random.fold_in(arg_keys[3], part), 4)
    voltages = noise(part_splits[0], (2, BEAMS, COARSE, UPCHAN, NT), 1.0, 6.0, ((2, 32),))
    sub_delays = draw_sub_delays(jax.random.fold_in(arg_keys[3], 71), part)
    merge_tables = draw_merge_tables(jax.random.fold_in(arg_keys[3], 71), part)
    return {"voltages": voltages, "sub_delays": sub_delays, "merge_tables": merge_tables}


epsilon = 1e-06

def window_table(tap_count, upchan):
    length = tap_count * upchan
    positions = jnp.arange(length, dtype=jnp.float32)
    window = jnp.sinc((positions - (length - 1) / 2.0) / upchan)
    window = window * (0.5 - 0.5 * jnp.cos(2.0 * math.pi * (positions + 0.5) / length))
    window = window / jnp.sqrt(2.0 * jnp.sum(window * window))
    return window.reshape(tap_count, upchan)

def filter_power(volts):
    signal = volts.astype(jnp.float32)
    upchan = signal.shape[3]
    samples = signal.shape[4]
    window = window_table(TAPS, upchan)
    padded = jnp.pad(signal, ((0, 0), (0, 0), (0, 0), (0, 0), (TAPS - 1, 0)))
    filtered = jnp.zeros_like(signal)
    for offset in range(TAPS):
        filtered = filtered + window[offset][:, None] * padded[..., TAPS - 1 - offset:TAPS - 1 - offset + samples]
    phase = jnp.arange(upchan, dtype=jnp.float32)
    angle = 2.0 * math.pi * phase[:, None] * phase[None, :] / upchan
    cosine = jnp.cos(angle)
    sine_table = jnp.sin(angle)
    high = lax.Precision.HIGHEST
    real_part = jnp.einsum('km,bcmt->bckt', cosine, filtered[0], precision=high) + jnp.einsum('km,bcmt->bckt', sine_table, filtered[1], precision=high)
    imag_part = jnp.einsum('km,bcmt->bckt', cosine, filtered[1], precision=high) - jnp.einsum('km,bcmt->bckt', sine_table, filtered[0], precision=high)
    intensity = (real_part * real_part + imag_part * imag_part).astype(jnp.bfloat16)
    return intensity.reshape(signal.shape[1], signal.shape[2] * upchan, samples)

def shift_rows(series, delays):
    samples = series.shape[-1]
    source_time = jnp.arange(samples, dtype=jnp.int32) - delays[..., None]
    inside = source_time >= 0
    source_time = jnp.broadcast_to(jnp.maximum(source_time, 0), series.shape)
    picked = jnp.take_along_axis(series, source_time, axis=-1)
    return jnp.where(jnp.broadcast_to(inside, series.shape), picked, jnp.zeros_like(picked))

def boxcar_peaks(series):
    samples = series.shape[-1]
    row_mean = lax.optimization_barrier(jnp.mean(series, axis=-1, keepdims=True))
    centred = series - row_mean
    inv_scale = lax.rsqrt(lax.optimization_barrier(jnp.mean(centred * centred, axis=-1, keepdims=True)) + epsilon)
    boxcar = centred * inv_scale
    maxima = [lax.optimization_barrier(jnp.max(boxcar, axis=-1))]
    span_now = 1
    for offset in range(1, WIDTHS):
        lagged = jnp.pad(boxcar[..., :samples - span_now], ((0, 0), (0, 0), (span_now, 0)))
        boxcar = boxcar + lagged
        span_now = span_now * 2
        maxima.append(lax.optimization_barrier(jnp.max(boxcar, axis=-1)) / math.sqrt(span_now))
    return jnp.stack(maxima, axis=1)

def reference(voltages, sub_delays, merge_tables):
    coarse_dev = COARSE // N_FREQ
    natural = voltages.reshape(2, BEAMS, N_FREQ, coarse_dev, UPCHAN, NT)
    natural = natural.transpose(0, 1, 3, 2, 4, 5).reshape(2, BEAMS, COARSE, UPCHAN, NT)
    intensity = filter_power(natural)
    chan_dev = COARSE * UPCHAN // N_FREQ
    grouped = intensity.reshape(BEAMS, N_FREQ, chan_dev, NT).astype(jnp.float32)
    padded = jnp.pad(grouped, ((0, 0), (0, 0), (0, 0), (SHIFTS - 1, 0)))
    delay_table = sub_delays.reshape(N_FREQ, DM_DEV, chan_dev)

    def add_shift(running, shift_now):
        onehot = (delay_table == shift_now).astype(jnp.float32)
        start = (SHIFTS - 1 - shift_now).astype(jnp.int32)
        shifted_block = lax.dynamic_slice_in_dim(padded, start, NT, 3)
        return (running + jnp.einsum('grc,bgct->bgrt', onehot, shifted_block, precision=lax.Precision.HIGHEST), None)
    merged, _ = lax.scan(add_shift, jnp.zeros((BEAMS, N_FREQ, DM_DEV, NT), jnp.float32), jnp.arange(SHIFTS, dtype=jnp.int32))
    devices = jnp.arange(N_FREQ, dtype=jnp.int32)
    for merge_level in range(LEVELS):
        tables_now = merge_tables[merge_level].reshape(3, N_FREQ, DM_DEV)
        upper_bit = devices // 2 ** merge_level % 2
        lower_device = devices - upper_bit * 2 ** merge_level
        upper_device = lower_device + 2 ** merge_level
        lower_term = merged[:, lower_device[:, None], tables_now[0], :]
        upper_term = merged[:, upper_device[:, None], tables_now[1], :]
        merged = lower_term + shift_rows(upper_term, tables_now[2])
    return boxcar_peaks(merged.reshape(BEAMS, N_FREQ * DM_DEV, NT))
```

```python
import functools
import math

import jax
import jax.numpy as jnp
import numpy as np
from jax import lax
from jax.experimental import pallas as pl
from jax.experimental.pallas import tpu as pltpu
from jax.sharding import PartitionSpec as P

TAPS = 4
WIDTHS = 8
SHIFTS = 32
INNER = 4

epsilon = 1e-06
f32 = jnp.float32
bf16 = jnp.bfloat16


def filter_matrix(upchan):
    length = TAPS * upchan
    n = np.arange(length, dtype=np.float64)
    window = np.sinc((n - (length - 1) / 2) / upchan) * (0.5 - 0.5 * np.cos(2 * np.pi * (n + 0.5) / length))
    window = (window / np.sqrt(2 * np.sum(window * window))).reshape(TAPS, upchan)
    phase = np.arange(upchan)
    angle = 2 * np.pi * (phase[:, None] * phase[None, :]) / upchan
    cosine, sine = np.cos(angle), np.sin(angle)
    transform = np.block([[cosine, sine], [-sine, cosine]])
    full = np.concatenate([transform * np.tile(window[tap], 2)[None, :] for tap in range(TAPS)], axis=1)
    pieces, rest = [], full
    for _ in range(3):
        piece = rest.astype(jnp.bfloat16)
        pieces.append(piece)
        rest = rest - piece.astype(np.float64)
    return np.concatenate(pieces, axis=0)


def shifted(x, amount):
    lane = lax.broadcasted_iota(jnp.int32, x.shape, 1)
    return jnp.where(lane >= amount, pltpu.roll(x, amount, 1), 0.0)


def filter_kernel(matrix_ref, volts_ref, out_ref):
    _, beams, count, upchan, samples = volts_ref.shape
    matrix = matrix_ref[...]
    rows = 2 * upchan
    for beam in range(beams):
        for q in range(count):
            x = volts_ref[:, beam, q].astype(f32).reshape(rows, samples)
            taps = [x] + [shifted(x, tap) for tap in range(1, TAPS)]
            stacked = jnp.concatenate(taps, axis=0).astype(bf16)
            y = jnp.dot(matrix, stacked, preferred_element_type=f32)
            y = y[:rows] + (y[rows : 2 * rows] + y[2 * rows :])
            power = y[:upchan] * y[:upchan] + y[upchan:] * y[upchan:]
            out_ref[q // 2, beam, q % 2] = power.astype(bf16)


def filter_power(voltages):
    parts, beams, coarse, upchan, samples = voltages.shape
    step = 8
    matrix = jnp.asarray(filter_matrix(upchan))
    return pl.pallas_call(
        filter_kernel,
        grid=(coarse // step,),
        out_shape=jax.ShapeDtypeStruct((coarse // 2, beams, 2, upchan, samples), bf16),
        in_specs=[
            pl.BlockSpec(matrix.shape, lambda i: (0, 0)),
            pl.BlockSpec((parts, beams, step, upchan, samples), lambda i: (0, 0, i, 0, 0)),
        ],
        out_specs=pl.BlockSpec((step // 2, beams, 2, upchan, samples), lambda i: (i, 0, 0, 0, 0)),
        name="filter_power",
    )(matrix, voltages)


def put_split(split_ref, slot, x):
    samples = x.shape[1]
    high = x.astype(bf16)
    split_ref[slot, :, :samples] = high
    split_ref[slot, :, samples:] = (x - high.astype(f32)).astype(bf16)


def table_columns(table, level):
    trials = table.shape[1]
    row = lax.broadcasted_iota(jnp.int32, (trials, trials), 0)
    lane = lax.broadcasted_iota(jnp.int32, (trials, trials), 1)
    eye = jnp.where(row == lane, 1.0, 0.0).astype(bf16)
    columns = lax.dot_general(eye, table.astype(bf16), (((1,), (1,)), ((), ())), preferred_element_type=f32)
    return columns[:, 3 * level : 3 * level + 3].astype(jnp.int32)


def take_rows(split, source):
    trials = split.shape[0]
    samples = split.shape[1] // 2
    lane = lax.broadcasted_iota(jnp.int32, (trials, trials), 1)
    onehot = jnp.where(lane == source, 1.0, 0.0).astype(bf16)
    y = jnp.dot(onehot, split, preferred_element_type=f32)
    return y[:, :samples] + y[:, samples:]


def delay_rows(x, delay):
    trials, samples = x.shape
    half = samples // 2
    lane = lax.broadcasted_iota(jnp.int32, (trials, half), 1)
    index = (lane - delay) & (half - 1)
    inside = lane >= delay
    first = jnp.take_along_axis(x[:, :half], index, axis=1)
    second = jnp.take_along_axis(x[:, half:], index, axis=1)
    return jnp.concatenate([jnp.where(inside, first, 0.0), jnp.where(inside, second, first)], axis=1)


def merge_unit(split_ref, table, level):
    columns = table_columns(table, level)
    lower = take_rows(split_ref[0], columns[:, 0:1])
    upper = take_rows(split_ref[1], columns[:, 1:2])
    return lower + delay_rows(upper, columns[:, 2:3])


def dedisperse_kernel(bits_ref, arrived_ref, delays_ref, tables_ref, kept_ref, sent_ref, stack_ref, split_ref, table_ref):
    sources, _, upchan, samples = arrived_ref.shape
    trials = delays_ref.shape[1]
    channels = sources * upchan
    core = bits_ref[0]
    for which in range(2):
        unit = core if which == 0 else 1 - core
        x = arrived_ref[:, pl.ds(unit, 1)].reshape(channels, samples).astype(f32)
        for inner in range(INNER):
            moved = x if inner == 0 else shifted(x, inner)
            stack_ref[inner * channels : (inner + 1) * channels] = moved.astype(bf16)
        delays = delays_ref[which]
        total = jnp.zeros((trials, samples), f32)
        for outer in reversed(range(SHIFTS // INNER)):
            onehot = jnp.concatenate(
                [
                    jnp.where(delays == jnp.asarray(outer * INNER + inner, bf16), jnp.asarray(1, bf16), jnp.asarray(0, bf16))
                    for inner in range(INNER)
                ],
                axis=1,
            )
            if outer != SHIFTS // INNER - 1:
                total = shifted(total, INNER)
            total = total + jnp.dot(onehot, stack_ref[...], preferred_element_type=f32)
        put_split(split_ref, unit, total)
        table_ref[unit] = tables_ref[which]
    emit(bits_ref[1], split_ref, table_ref, 0, kept_ref, sent_ref)


def emit(keep, split_ref, table_ref, level, kept_ref, sent_ref):
    trials = split_ref.shape[1]
    for out_ref, unit in ((sent_ref, 1 - keep), (kept_ref, keep)):
        table = table_ref[unit]
        out_ref[:trials] = merge_unit(split_ref, table, level)
        out_ref[trials:] = table


def merge_kernel(level, bits_ref, kept_in_ref, received_ref, kept_ref, sent_ref, split_ref, table_ref):
    load_units(bits_ref[level], kept_in_ref, received_ref, split_ref, table_ref)
    emit(bits_ref[level + 1], split_ref, table_ref, level, kept_ref, sent_ref)


def load_units(own, kept_in_ref, received_ref, split_ref, table_ref):
    trials = split_ref.shape[1]
    for in_ref, unit in ((kept_in_ref, own), (received_ref, 1 - own)):
        put_split(split_ref, unit, in_ref[:trials])
        table_ref[unit] = in_ref[trials:]


def peaks_kernel(level, bits_ref, kept_in_ref, received_ref, out_ref, split_ref, table_ref):
    load_units(bits_ref[level], kept_in_ref, received_ref, split_ref, table_ref)
    for slot in range(2):
        unit = bits_ref[0] if slot == 0 else 1 - bits_ref[0]
        merged = merge_unit(split_ref, table_ref[unit], level)
        series = merged.T
        samples = series.shape[0]
        mean = jnp.sum(series, axis=0, keepdims=True) * (1.0 / samples)
        centred = series - mean
        variance = jnp.sum(centred * centred, axis=0, keepdims=True) * (1.0 / samples)
        boxcar = centred * lax.rsqrt(variance + epsilon)
        peaks = [jnp.max(boxcar, axis=0, keepdims=True)]
        width = 1
        for _ in range(1, WIDTHS):
            row = lax.broadcasted_iota(jnp.int32, boxcar.shape, 0)
            boxcar = boxcar + jnp.where(row >= width, pltpu.roll(boxcar, width, 0), 0.0)
            width *= 2
            peaks.append(jnp.max(boxcar, axis=0, keepdims=True) * (1.0 / math.sqrt(width)))
        out_ref[slot] = jnp.concatenate(peaks, axis=0)


VMEM = pl.BlockSpec(memory_space=pltpu.VMEM)
SMEM = pl.BlockSpec(memory_space=pltpu.SMEM)


def unit_scratch(trials, samples, table_rows):
    return [pltpu.VMEM((2, trials, 2 * samples), bf16), pltpu.VMEM((2, table_rows, samples), f32)]


def swap(x, bit):
    return lax.ppermute(x, "freq", [(i, i ^ (1 << bit)) for i in range(lax.axis_size("freq"))])


def local(voltages, sub_delays, merge_tables):
    freq_count = lax.axis_size("freq")
    levels = freq_count.bit_length() - 1
    trials, channels = sub_delays.shape
    samples = voltages.shape[4]
    upchan = voltages.shape[3]
    position = lax.axis_index("freq")
    bits = (position >> jnp.arange(8, dtype=jnp.int32)) & 1

    power = filter_power(voltages)
    power = power.reshape(freq_count, 2, upchan, samples)
    arrived = lax.all_to_all(power, "freq", split_axis=0, concat_axis=0, tiled=True)

    delays = sub_delays.astype(bf16)
    delays = jnp.stack([delays, swap(delays, 0)])
    tables = merge_tables.reshape(3 * levels, trials).astype(f32)
    tables = jnp.pad(tables, ((0, -3 * levels % 8), (0, 0)))
    tables = jnp.stack([tables, swap(tables, 0)])
    table_rows = tables.shape[1]

    message = jax.ShapeDtypeStruct((trials + table_rows, samples), f32)
    scratch = unit_scratch(trials, samples, table_rows)
    kept, sent = pl.pallas_call(
        dedisperse_kernel,
        out_shape=(message, message),
        in_specs=[SMEM, VMEM, VMEM, VMEM],
        out_specs=(VMEM, VMEM),
        scratch_shapes=[pltpu.VMEM((INNER * channels, samples), bf16)] + scratch,
        name="dedisperse",
    )(bits, arrived, delays, tables)
    for level in range(1, levels):
        received = swap(sent, level)
        if level < levels - 1:
            kept, sent = pl.pallas_call(
                functools.partial(merge_kernel, level),
                out_shape=(message, message),
                in_specs=[SMEM, VMEM, VMEM],
                out_specs=(VMEM, VMEM),
                scratch_shapes=scratch,
                name="merge",
            )(bits, kept, received)
    peaks = pl.pallas_call(
        functools.partial(peaks_kernel, levels - 1),
        out_shape=jax.ShapeDtypeStruct((2, WIDTHS, trials), f32),
        in_specs=[SMEM, VMEM, VMEM],
        out_specs=VMEM,
        scratch_shapes=scratch,
        name="peaks",
    )(bits, kept, received)
    half = freq_count // 2
    first = lax.ppermute(peaks[0], "freq", [(d, (d & 1) * half + (d >> 1)) for d in range(freq_count)])
    second = lax.ppermute(peaks[1], "freq", [(d, (1 - (d & 1)) * half + (d >> 1)) for d in range(freq_count)])
    top = bits[levels - 1] == 1
    return jnp.stack([jnp.where(top, second, first), jnp.where(top, first, second)])


def solution(mesh):
    return jax.shard_map(
        local,
        mesh=mesh,
        in_specs=(P(None, "beam", "freq", None, None), P("freq", None), P(None, None, "freq")),
        out_specs=P("beam", None, "freq"),
        check_vma=False,
    )
```

```python
import functools
import math

import jax
import jax.numpy as jnp
import numpy as np
from jax import lax
from jax.experimental import pallas as pl
from jax.experimental.pallas import tpu as pltpu
from jax.sharding import PartitionSpec as P

TAPS = 4
WIDTHS = 8
SHIFTS = 32
INNER = 4

epsilon = 1e-06
f32 = jnp.float32
bf16 = jnp.bfloat16


def filter_matrix(upchan):
    length = TAPS * upchan
    n = np.arange(length, dtype=np.float64)
    window = np.sinc((n - (length - 1) / 2) / upchan) * (0.5 - 0.5 * np.cos(2 * np.pi * (n + 0.5) / length))
    window = (window / np.sqrt(2 * np.sum(window * window))).reshape(TAPS, upchan)
    phase = np.arange(upchan)
    angle = 2 * np.pi * (phase[:, None] * phase[None, :]) / upchan
    cosine, sine = np.cos(angle), np.sin(angle)
    transform = np.block([[cosine, sine], [-sine, cosine]])
    full = np.concatenate([transform * np.tile(window[tap], 2)[None, :] for tap in range(TAPS)], axis=1)
    pieces, rest = [], full
    for _ in range(3):
        piece = rest.astype(jnp.bfloat16)
        pieces.append(piece)
        rest = rest - piece.astype(np.float64)
    return np.concatenate(pieces, axis=0)


def shifted(x, amount):
    lane = lax.broadcasted_iota(jnp.int32, x.shape, 1)
    return jnp.where(lane >= amount, pltpu.roll(x, amount, 1), 0.0)


def filter_kernel(matrix_ref, volts_ref, out_ref):
    _, beams, count, upchan, samples = volts_ref.shape
    matrix = matrix_ref[...]
    rows = 2 * upchan
    for beam in range(beams):
        for q in range(count):
            x = volts_ref[:, beam, q].astype(f32).reshape(rows, samples)
            taps = [x] + [shifted(x, tap) for tap in range(1, TAPS)]
            stacked = jnp.concatenate(taps, axis=0).astype(bf16)
            y = jnp.dot(matrix, stacked, preferred_element_type=f32)
            y = y[:rows] + (y[rows : 2 * rows] + y[2 * rows :])
            power = y[:upchan] * y[:upchan] + y[upchan:] * y[upchan:]
            out_ref[q // 2, beam, q % 2] = power.astype(bf16)


def filter_power(voltages):
    parts, beams, coarse, upchan, samples = voltages.shape
    step = 8
    matrix = jnp.asarray(filter_matrix(upchan))
    return pl.pallas_call(
        filter_kernel,
        grid=(coarse // step,),
        out_shape=jax.ShapeDtypeStruct((coarse // 2, beams, 2, upchan, samples), bf16),
        in_specs=[
            pl.BlockSpec(matrix.shape, lambda i: (0, 0)),
            pl.BlockSpec((parts, beams, step, upchan, samples), lambda i: (0, 0, i, 0, 0)),
        ],
        out_specs=pl.BlockSpec((step // 2, beams, 2, upchan, samples), lambda i: (i, 0, 0, 0, 0)),
        compiler_params=pltpu.CompilerParams(vmem_limit_bytes=8 << 20),
        name="filter_power",
    )(matrix, voltages)


def split_of(x):
    high = x.astype(bf16)
    return jnp.concatenate([high, (x - high.astype(f32)).astype(bf16)], axis=1)


def eye_mask(size):
    row = lax.broadcasted_iota(jnp.int32, (size, size), 0)
    return row == lax.broadcasted_iota(jnp.int32, (size, size), 1)


def columns_of(table):
    eye = jnp.where(eye_mask(table.shape[1]), 1.0, 0.0).astype(bf16)
    columns = lax.dot_general(eye, table.astype(bf16), (((1,), (1,)), ((), ())), preferred_element_type=f32)
    return columns.astype(jnp.int32)


def take_rows(split, source):
    trials = split.shape[0]
    samples = split.shape[1] // 2
    lane = lax.broadcasted_iota(jnp.int32, (trials, trials), 1)
    onehot = jnp.where(lane == source, 1.0, 0.0).astype(bf16)
    y = jnp.dot(onehot, split, preferred_element_type=f32)
    return y[:, :samples] + y[:, samples:]


def delay_rows(x, delay):
    trials, samples = x.shape
    half = samples // 2
    lane = lax.broadcasted_iota(jnp.int32, (trials, half), 1)
    index = (lane - delay) & (half - 1)
    inside = lane >= delay
    first = jnp.take_along_axis(x[:, :half], index, axis=1)
    second = jnp.take_along_axis(x[:, half:], index, axis=1)
    return jnp.concatenate([jnp.where(inside, first, 0.0), jnp.where(inside, second, first)], axis=1)


def merge_unit(split_ref, table, level):
    columns = columns_of(table)
    lower = take_rows(split_ref[0], columns[:, 3 * level : 3 * level + 1])
    upper = take_rows(split_ref[1], columns[:, 3 * level + 1 : 3 * level + 2])
    return lower + delay_rows(upper, columns[:, 3 * level + 2 : 3 * level + 3])


STEPS = 65534.0


def put_message(out_ref, x, table):
    trials = x.shape[0]
    peak = jnp.maximum(jnp.max(x, axis=1, keepdims=True), 1e-30)
    code = jnp.floor(jnp.log2(peak) * 256.0) + 2.0
    scale = jnp.exp2(code * (-1.0 / 256.0)) * STEPS
    out_ref[:trials] = ((x * scale + 0.5).astype(jnp.int32) - int(STEPS) // 2).astype(jnp.int16)
    code_row = jnp.sum(jnp.where(eye_mask(trials), code, 0.0), axis=0, keepdims=True).astype(jnp.int32)
    row = lax.broadcasted_iota(jnp.int32, table.shape, 0)
    rows = jnp.where(row == 0, code_row >> 8, jnp.where(row == 1, code_row & 255, table.astype(jnp.int32)))
    out_ref[trials:] = rows.astype(jnp.int16)


def take_message(in_ref, trials):
    table = in_ref[trials:].astype(jnp.int32).astype(f32)
    columns = columns_of(table)
    code = (columns[:, 0:1] * 256 + columns[:, 1:2]).astype(f32)
    scale = jnp.exp2(code * (1.0 / 256.0)) * (1.0 / STEPS)
    x = (in_ref[:trials].astype(jnp.int32) + int(STEPS) // 2).astype(f32) * scale
    return x, table


def dedisperse_kernel(bits_ref, arrived_ref, delays_ref, tables_ref, sent_ref, split_ref, table_ref, stack_ref):
    sources, _, upchan, samples = arrived_ref.shape
    trials = delays_ref.shape[1]
    channels = sources * upchan
    core = bits_ref[0]
    for which in range(2):
        unit = core if which == 0 else 1 - core
        x = arrived_ref[:, pl.ds(unit, 1)].reshape(channels, samples).astype(f32)
        for inner in range(INNER):
            moved = x if inner == 0 else shifted(x, inner)
            stack_ref[inner * channels : (inner + 1) * channels] = moved.astype(bf16)
        delays = delays_ref[which]
        total = jnp.zeros((trials, samples), f32)
        for outer in reversed(range(SHIFTS // INNER)):
            onehot = jnp.concatenate(
                [
                    jnp.where(delays == jnp.asarray(outer * INNER + inner, bf16), jnp.asarray(1, bf16), jnp.asarray(0, bf16))
                    for inner in range(INNER)
                ],
                axis=1,
            )
            if outer != SHIFTS // INNER - 1:
                total = shifted(total, INNER)
            total = total + jnp.dot(onehot, stack_ref[...], preferred_element_type=f32)
        split_ref[unit] = split_of(total)
        table_ref[unit] = tables_ref[which]
    put_sent(0, bits_ref, split_ref, table_ref, sent_ref)


def put_sent(level, bits_ref, split_ref, table_ref, sent_ref):
    table = table_ref[1 - bits_ref[level + 1]]
    put_message(sent_ref, merge_unit(split_ref, table, level), table)


def kept_kernel(level, bits_ref, split_in_ref, table_in_ref, split_ref, table_ref):
    table = table_in_ref[bits_ref[level + 1]]
    split_ref[...] = split_of(merge_unit(split_in_ref, table, level))
    table_ref[...] = table


def load_units(own, kept_split_ref, kept_table_ref, received_ref, split_ref, table_ref):
    split_ref[own] = kept_split_ref[...]
    table_ref[own] = kept_table_ref[...]
    x, table = take_message(received_ref, kept_split_ref.shape[0])
    split_ref[1 - own] = split_of(x)
    table_ref[1 - own] = table


def sent_kernel(level, bits_ref, kept_split_ref, kept_table_ref, received_ref, sent_ref, split_ref, table_ref):
    load_units(bits_ref[level], kept_split_ref, kept_table_ref, received_ref, split_ref, table_ref)
    put_sent(level, bits_ref, split_ref, table_ref, sent_ref)


def peaks_kernel(level, bits_ref, kept_split_ref, kept_table_ref, received_ref, first_ref, second_ref, split_ref, table_ref):
    load_units(bits_ref[level], kept_split_ref, kept_table_ref, received_ref, split_ref, table_ref)
    for out_ref, unit in ((first_ref, bits_ref[0]), (second_ref, 1 - bits_ref[0])):
        merged = merge_unit(split_ref, table_ref[unit], level)
        series = merged.T
        samples = series.shape[0]
        mean = jnp.sum(series, axis=0, keepdims=True) * (1.0 / samples)
        centred = series - mean
        variance = jnp.sum(centred * centred, axis=0, keepdims=True) * (1.0 / samples)
        boxcar = centred * lax.rsqrt(variance + epsilon)
        peaks = [jnp.max(boxcar, axis=0, keepdims=True)]
        width = 1
        for _ in range(1, WIDTHS):
            row = lax.broadcasted_iota(jnp.int32, boxcar.shape, 0)
            boxcar = boxcar + jnp.where(row >= width, pltpu.roll(boxcar, width, 0), 0.0)
            width *= 2
            peaks.append(jnp.max(boxcar, axis=0, keepdims=True) * (1.0 / math.sqrt(width)))
        out_ref[...] = jnp.concatenate(peaks, axis=0)


def join_kernel(level, bits_ref, first_ref, second_ref, out_ref):
    out_ref[bits_ref[level]] = first_ref[...]
    out_ref[1 - bits_ref[level]] = second_ref[...]


VMEM = pl.BlockSpec(memory_space=pltpu.VMEM)
SMEM = pl.BlockSpec(memory_space=pltpu.SMEM)


def call(kernel, name, outs, operands, scratch=(), mebibytes=8):
    return pl.pallas_call(
        kernel,
        out_shape=tuple(jax.ShapeDtypeStruct(shape, dtype) for shape, dtype in outs),
        in_specs=[SMEM] + [VMEM] * (len(operands) - 1),
        out_specs=tuple(VMEM for _ in outs),
        scratch_shapes=list(scratch),
        compiler_params=pltpu.CompilerParams(vmem_limit_bytes=mebibytes << 20),
        name=name,
    )(*operands)


def swap(x, bit):
    return lax.ppermute(x, "freq", [(i, i ^ (1 << bit)) for i in range(lax.axis_size("freq"))])


def local(voltages, sub_delays, merge_tables):
    freq_count = lax.axis_size("freq")
    levels = freq_count.bit_length() - 1
    trials, channels = sub_delays.shape
    samples = voltages.shape[4]
    upchan = voltages.shape[3]
    position = lax.axis_index("freq")
    bits = (position >> jnp.arange(8, dtype=jnp.int32)) & 1

    power = filter_power(voltages)
    power = power.reshape(freq_count, 2, upchan, samples)
    arrived = lax.all_to_all(power, "freq", split_axis=0, concat_axis=0, tiled=True)

    delays = sub_delays.astype(bf16)
    delays = jnp.stack([delays, swap(delays, 0)])
    tables = merge_tables.reshape(3 * levels, trials).astype(f32)
    tables = jnp.pad(tables, ((0, -3 * levels % 16), (0, 0)))
    tables = jnp.stack([tables, swap(tables, 0)])
    rows = tables.shape[1]

    message = ((trials + rows, samples), jnp.int16)
    splits, both_tables = ((2, trials, 2 * samples), bf16), ((2, rows, samples), f32)
    split, table = ((trials, 2 * samples), bf16), ((rows, samples), f32)
    stack = pltpu.VMEM((INNER * channels, samples), bf16)
    sent, *both = call(
        dedisperse_kernel, "dedisperse", (message, splits, both_tables), (bits, arrived, delays, tables), [stack], 24
    )
    for level in range(levels - 1):
        received = swap(sent, level + 1)
        kept = call(functools.partial(kept_kernel, level), "kept", (split, table), (bits, *both))
        if level < levels - 2:
            sent, *both = call(
                functools.partial(sent_kernel, level + 1), "sent", (message, splits, both_tables), (bits, *kept, received)
            )
    peak = ((WIDTHS, trials), f32)
    scratch = [pltpu.VMEM(*splits), pltpu.VMEM(*both_tables)]
    first, second = call(
        functools.partial(peaks_kernel, levels - 1), "peaks", (peak, peak), (bits, *kept, received), scratch
    )
    half = freq_count // 2
    first = lax.ppermute(first, "freq", [(d, (d & 1) * half + (d >> 1)) for d in range(freq_count)])
    second = lax.ppermute(second, "freq", [(d, (1 - (d & 1)) * half + (d >> 1)) for d in range(freq_count)])
    return call(
        functools.partial(join_kernel, levels - 1), "join", (((2, WIDTHS, trials), f32),), (bits, first, second)
    )[0]


def solution(mesh):
    return jax.shard_map(
        local,
        mesh=mesh,
        in_specs=(P(None, "beam", "freq", None, None), P("freq", None), P(None, None, "freq")),
        out_specs=P("beam", None, "freq"),
        check_vma=False,
    )
```

```python
import functools
import math

import jax
import jax.numpy as jnp
import numpy as np
from jax import lax
from jax.experimental import pallas as pl
from jax.experimental.pallas import tpu as pltpu
from jax.sharding import PartitionSpec as P

TAPS = 4
WIDTHS = 8
SHIFTS = 32
INNER = 4

BEAM_BIT = 2
SWAP_BITS = (0, 1, 3, 4)

epsilon = 1e-06
f32 = jnp.float32
bf16 = jnp.bfloat16


def filter_matrix(upchan):
    length = TAPS * upchan
    n = np.arange(length, dtype=np.float64)
    window = np.sinc((n - (length - 1) / 2) / upchan) * (0.5 - 0.5 * np.cos(2 * np.pi * (n + 0.5) / length))
    window = (window / np.sqrt(2 * np.sum(window * window))).reshape(TAPS, upchan)
    phase = np.arange(upchan)
    angle = 2 * np.pi * (phase[:, None] * phase[None, :]) / upchan
    cosine, sine = np.cos(angle), np.sin(angle)
    transform = np.block([[cosine, sine], [-sine, cosine]])
    full = np.concatenate([transform * np.tile(window[tap], 2)[None, :] for tap in range(TAPS)], axis=1)
    pieces, rest = [], full
    for _ in range(3):
        piece = rest.astype(jnp.bfloat16)
        pieces.append(piece)
        rest = rest - piece.astype(np.float64)
    return np.concatenate(pieces, axis=0)


def shifted(x, amount):
    lane = lax.broadcasted_iota(jnp.int32, x.shape, 1)
    return jnp.where(lane >= amount, pltpu.roll(x, amount, 1), 0.0)


def filter_kernel(matrix_ref, volts_ref, out_ref):
    _, beams, count, upchan, samples = volts_ref.shape
    matrix = matrix_ref[...]
    rows = 2 * upchan
    for beam in range(beams):
        for q in range(count):
            x = volts_ref[:, beam, q].astype(f32).reshape(rows, samples)
            taps = [x] + [shifted(x, tap) for tap in range(1, TAPS)]
            stacked = jnp.concatenate(taps, axis=0).astype(bf16)
            y = jnp.dot(matrix, stacked, preferred_element_type=f32)
            y = y[:rows] + (y[rows : 2 * rows] + y[2 * rows :])
            power = y[:upchan] * y[:upchan] + y[upchan:] * y[upchan:]
            out_ref[q // 2 + beam * (count // 2), q % 2] = power.astype(bf16)


def filter_power(voltages):
    parts, beams, coarse, upchan, samples = voltages.shape
    step = 2 << BEAM_BIT
    matrix = jnp.asarray(filter_matrix(upchan))
    return pl.pallas_call(
        filter_kernel,
        grid=(coarse // step,),
        out_shape=jax.ShapeDtypeStruct((coarse // 2 * beams, 2, upchan, samples), bf16),
        in_specs=[
            pl.BlockSpec(matrix.shape, lambda i: (0, 0)),
            pl.BlockSpec((parts, beams, step, upchan, samples), lambda i: (0, 0, i, 0, 0)),
        ],
        out_specs=pl.BlockSpec((step // 2 * beams, 2, upchan, samples), lambda i: (i, 0, 0, 0)),
        name="filter_power",
    )(matrix, voltages)


def split_of(x):
    high = x.astype(bf16)
    return jnp.concatenate([high, (x - high.astype(f32)).astype(bf16)], axis=1)


def eye_mask(size):
    row = lax.broadcasted_iota(jnp.int32, (size, size), 0)
    return row == lax.broadcasted_iota(jnp.int32, (size, size), 1)


def columns_of(table):
    eye = jnp.where(eye_mask(table.shape[1]), 1.0, 0.0).astype(bf16)
    columns = lax.dot_general(eye, table.astype(bf16), (((1,), (1,)), ((), ())), preferred_element_type=f32)
    return columns.astype(jnp.int32)


def take_rows(split, source):
    trials = split.shape[0]
    samples = split.shape[1] // 2
    lane = lax.broadcasted_iota(jnp.int32, (trials, trials), 1)
    onehot = jnp.where(lane == source, 1.0, 0.0).astype(bf16)
    y = jnp.dot(onehot, split, preferred_element_type=f32)
    return y[:, :samples] + y[:, samples:]


def delay_rows(x, delay):
    trials, samples = x.shape
    half = samples // 2
    lane = lax.broadcasted_iota(jnp.int32, (trials, half), 1)
    index = (lane - delay) & (half - 1)
    inside = lane >= delay
    first = jnp.take_along_axis(x[:, :half], index, axis=1)
    second = jnp.take_along_axis(x[:, half:], index, axis=1)
    return jnp.concatenate([jnp.where(inside, first, 0.0), jnp.where(inside, second, first)], axis=1)


def merge_unit(split_ref, table, level):
    columns = columns_of(table)
    lower = take_rows(split_ref[0], columns[:, 3 * level : 3 * level + 1])
    upper = take_rows(split_ref[1], columns[:, 3 * level + 1 : 3 * level + 2])
    return lower + delay_rows(upper, columns[:, 3 * level + 2 : 3 * level + 3])


STEPS = 65534.0


def put_message(out_ref, x, table):
    trials = x.shape[0]
    peak = jnp.maximum(jnp.max(x, axis=1, keepdims=True), 1e-30)
    code = jnp.floor(jnp.log2(peak) * 256.0) + 2.0
    scale = jnp.exp2(code * (-1.0 / 256.0)) * STEPS
    out_ref[:trials] = ((x * scale + 0.5).astype(jnp.int32) - int(STEPS) // 2).astype(jnp.int16)
    code_row = jnp.sum(jnp.where(eye_mask(trials), code, 0.0), axis=0, keepdims=True).astype(jnp.int32)
    row = lax.broadcasted_iota(jnp.int32, table.shape, 0)
    rows = jnp.where(row == 0, code_row >> 8, jnp.where(row == 1, code_row & 255, table.astype(jnp.int32)))
    out_ref[trials:] = rows.astype(jnp.int16)


def take_message(in_ref, trials):
    table = in_ref[trials:].astype(jnp.int32).astype(f32)
    columns = columns_of(table)
    code = (columns[:, 0:1] * 256 + columns[:, 1:2]).astype(f32)
    scale = jnp.exp2(code * (1.0 / 256.0)) * (1.0 / STEPS)
    x = (in_ref[:trials].astype(jnp.int32) + int(STEPS) // 2).astype(f32) * scale
    return x, table


def dedisperse_kernel(bits_ref, arrived_ref, delays_ref, tables_ref, sent_ref, split_ref, table_ref, stack_ref):
    sources, _, upchan, samples = arrived_ref.shape
    trials = delays_ref.shape[1]
    channels = sources * upchan
    first = bits_ref[BEAM_BIT]
    for which in range(2):
        unit = first if which == 0 else 1 - first
        x = arrived_ref[:, pl.ds(unit, 1)].reshape(channels, samples).astype(f32)
        for inner in range(INNER):
            moved = x if inner == 0 else shifted(x, inner)
            stack_ref[inner * channels : (inner + 1) * channels] = moved.astype(bf16)
        delays = delays_ref[which]
        total = jnp.zeros((trials, samples), f32)
        for outer in reversed(range(SHIFTS // INNER)):
            onehot = jnp.concatenate(
                [
                    jnp.where(delays == jnp.asarray(outer * INNER + inner, bf16), jnp.asarray(1, bf16), jnp.asarray(0, bf16))
                    for inner in range(INNER)
                ],
                axis=1,
            )
            if outer != SHIFTS // INNER - 1:
                total = shifted(total, INNER)
            total = total + jnp.dot(onehot, stack_ref[...], preferred_element_type=f32)
        split_ref[unit] = split_of(total)
        table_ref[unit] = tables_ref[which]
    put_sent(0, bits_ref, split_ref, table_ref, sent_ref)


def put_sent(level, bits_ref, split_ref, table_ref, sent_ref):
    table = table_ref[1 - bits_ref[SWAP_BITS[level]]]
    put_message(sent_ref, merge_unit(split_ref, table, level), table)


def kept_kernel(level, bits_ref, split_in_ref, table_in_ref, split_ref, table_ref):
    table = table_in_ref[bits_ref[SWAP_BITS[level]]]
    split_ref[...] = split_of(merge_unit(split_in_ref, table, level))
    table_ref[...] = table


def load_units(own, kept_split_ref, kept_table_ref, received_ref, split_ref, table_ref):
    split_ref[own] = kept_split_ref[...]
    table_ref[own] = kept_table_ref[...]
    x, table = take_message(received_ref, kept_split_ref.shape[0])
    split_ref[1 - own] = split_of(x)
    table_ref[1 - own] = table


def sent_kernel(level, bits_ref, kept_split_ref, kept_table_ref, received_ref, sent_ref, split_ref, table_ref):
    load_units(bits_ref[SWAP_BITS[level - 1]], kept_split_ref, kept_table_ref, received_ref, split_ref, table_ref)
    put_sent(level, bits_ref, split_ref, table_ref, sent_ref)


def peaks_kernel(level, bits_ref, kept_split_ref, kept_table_ref, received_ref, first_ref, second_ref, split_ref, table_ref):
    load_units(bits_ref[SWAP_BITS[level - 1]], kept_split_ref, kept_table_ref, received_ref, split_ref, table_ref)
    for out_ref, unit in ((first_ref, bits_ref[BEAM_BIT]), (second_ref, 1 - bits_ref[BEAM_BIT])):
        merged = merge_unit(split_ref, table_ref[unit], level)
        series = merged.T
        samples = series.shape[0]
        mean = jnp.sum(series, axis=0, keepdims=True) * (1.0 / samples)
        centred = series - mean
        variance = jnp.sum(centred * centred, axis=0, keepdims=True) * (1.0 / samples)
        boxcar = centred * lax.rsqrt(variance + epsilon)
        peaks = [jnp.max(boxcar, axis=0, keepdims=True)]
        width = 1
        for _ in range(1, WIDTHS):
            row = lax.broadcasted_iota(jnp.int32, boxcar.shape, 0)
            boxcar = boxcar + jnp.where(row >= width, pltpu.roll(boxcar, width, 0), 0.0)
            width *= 2
            peaks.append(jnp.max(boxcar, axis=0, keepdims=True) * (1.0 / math.sqrt(width)))
        out_ref[...] = jnp.concatenate(peaks, axis=0)


def join_kernel(level, bits_ref, first_ref, second_ref, out_ref):
    out_ref[bits_ref[level]] = first_ref[...]
    out_ref[1 - bits_ref[level]] = second_ref[...]


VMEM = pl.BlockSpec(memory_space=pltpu.VMEM)
SMEM = pl.BlockSpec(memory_space=pltpu.SMEM)


def call(kernel, name, outs, operands, scratch=(), mebibytes=8):
    return pl.pallas_call(
        kernel,
        out_shape=tuple(jax.ShapeDtypeStruct(shape, dtype) for shape, dtype in outs),
        in_specs=[SMEM] + [VMEM] * (len(operands) - 1),
        out_specs=tuple(VMEM for _ in outs),
        scratch_shapes=list(scratch),
        compiler_params=pltpu.CompilerParams(vmem_limit_bytes=mebibytes << 20),
        name=name,
    )(*operands)


def move(x, target):
    return lax.ppermute(x, "freq", [(i, target(i)) for i in range(lax.axis_size("freq"))])


def swap(x, bit):
    return move(x, lambda i: i ^ (1 << bit))


def bit(number, index):
    return number >> index & 1


def gather_units(x):
    def target(flip):
        def device(g):
            low = g >> 1 & (1 << BEAM_BIT) - 1
            return low | (bit(g, 0) ^ flip) << BEAM_BIT | g >> (BEAM_BIT + 1) << (BEAM_BIT + 1)

        return device

    return jnp.stack([move(x, target(0)), move(x, target(1))])


def home(flip, top):
    def device(d):
        low = d & (1 << BEAM_BIT) - 1
        return low | d >> (BEAM_BIT + 1) << BEAM_BIT | (bit(d, BEAM_BIT) ^ flip) << top

    return device


def local(voltages, sub_delays, merge_tables):
    freq_count = lax.axis_size("freq")
    levels = freq_count.bit_length() - 1
    trials, channels = sub_delays.shape
    samples = voltages.shape[4]
    upchan = voltages.shape[3]
    position = lax.axis_index("freq")
    bits = (position >> jnp.arange(8, dtype=jnp.int32)) & 1

    power = filter_power(voltages)
    power = power.reshape(freq_count, 2, upchan, samples)
    arrived = lax.all_to_all(power, "freq", split_axis=0, concat_axis=0, tiled=True)

    delays = sub_delays.astype(bf16)
    delays = gather_units(delays)
    tables = merge_tables.reshape(3 * levels, trials).astype(f32)
    tables = jnp.pad(tables, ((0, -3 * levels % 16), (0, 0)))
    tables = gather_units(tables)
    rows = tables.shape[1]

    message = ((trials + rows, samples), jnp.int16)
    splits, both_tables = ((2, trials, 2 * samples), bf16), ((2, rows, samples), f32)
    split, table = ((trials, 2 * samples), bf16), ((rows, samples), f32)
    stack = pltpu.VMEM((INNER * channels, samples), bf16)
    sent, *both = call(
        dedisperse_kernel, "dedisperse", (message, splits, both_tables), (bits, arrived, delays, tables), [stack], 24
    )
    for level in range(levels - 1):
        received = swap(sent, SWAP_BITS[level])
        kept = call(functools.partial(kept_kernel, level), "kept", (split, table), (bits, *both))
        if level < levels - 2:
            sent, *both = call(
                functools.partial(sent_kernel, level + 1), "sent", (message, splits, both_tables), (bits, *kept, received)
            )
    peak = ((WIDTHS, trials), f32)
    scratch = [pltpu.VMEM(*splits), pltpu.VMEM(*both_tables)]
    first, second = call(
        functools.partial(peaks_kernel, levels - 1), "peaks", (peak, peak), (bits, *kept, received), scratch
    )
    first, second = move(first, home(0, levels - 1)), move(second, home(1, levels - 1))
    return call(
        functools.partial(join_kernel, levels - 1), "join", (((2, WIDTHS, trials), f32),), (bits, first, second)
    )[0]


def solution(mesh):
    return jax.shard_map(
        local,
        mesh=mesh,
        in_specs=(P(None, "beam", "freq", None, None), P("freq", None), P(None, None, "freq")),
        out_specs=P("beam", None, "freq"),
        check_vma=False,
    )
```

```python
import functools
import math

import jax
import jax.numpy as jnp
import numpy as np
from jax import lax
from jax.experimental import pallas as pl
from jax.experimental.pallas import tpu as pltpu
from jax.sharding import PartitionSpec as P

TAPS = 4
WIDTHS = 8
SHIFTS = 32
INNER = 4

BEAM_BIT = 2
SWAP_BITS = (0, 1, 3, 4)

epsilon = 1e-06
f32 = jnp.float32
bf16 = jnp.bfloat16


def filter_matrix(upchan):
    length = TAPS * upchan
    n = np.arange(length, dtype=np.float64)
    window = np.sinc((n - (length - 1) / 2) / upchan) * (0.5 - 0.5 * np.cos(2 * np.pi * (n + 0.5) / length))
    window = (window / np.sqrt(2 * np.sum(window * window))).reshape(TAPS, upchan)
    phase = np.arange(upchan)
    angle = 2 * np.pi * (phase[:, None] * phase[None, :]) / upchan
    cosine, sine = np.cos(angle), np.sin(angle)
    transform = np.block([[cosine, sine], [-sine, cosine]])
    full = np.concatenate([transform * np.tile(window[tap], 2)[None, :] for tap in range(TAPS)], axis=1)
    pieces, rest = [], full
    for _ in range(2):
        piece = rest.astype(jnp.bfloat16)
        pieces.append(piece)
        rest = rest - piece.astype(np.float64)
    return np.concatenate(pieces, axis=0)


def shifted(x, amount):
    lane = lax.broadcasted_iota(jnp.int32, x.shape, 1)
    return jnp.where(lane >= amount, pltpu.roll(x, amount, 1), 0.0)


def filter_kernel(matrix_ref, volts_ref, out_ref):
    _, beams, count, upchan, samples = volts_ref.shape
    matrix = matrix_ref[...]
    rows = 2 * upchan
    for beam in range(beams):
        for q in range(count):
            x = volts_ref[:, beam, q].astype(f32).reshape(rows, samples)
            taps = [x] + [shifted(x, tap) for tap in range(1, TAPS)]
            stacked = jnp.concatenate(taps, axis=0).astype(bf16)
            y = jnp.dot(matrix, stacked, preferred_element_type=f32)
            y = y[:rows] + y[rows:]
            power = y[:upchan] * y[:upchan] + y[upchan:] * y[upchan:]
            out_ref[0, beam, 0, q // 2, q % 2] = power.astype(bf16)


def filter_power(voltages):
    parts, beams, coarse, upchan, samples = voltages.shape
    step = 1 << BEAM_BIT
    matrix = jnp.asarray(filter_matrix(upchan))
    power = pl.pallas_call(
        filter_kernel,
        grid=(coarse // step,),
        out_shape=jax.ShapeDtypeStruct((coarse // step // 2, beams, 2, step // 2, 2, upchan, samples), bf16),
        in_specs=[
            pl.BlockSpec(matrix.shape, lambda i: (0, 0)),
            pl.BlockSpec((parts, beams, step, upchan, samples), lambda i: (0, 0, i, 0, 0)),
        ],
        out_specs=pl.BlockSpec((1, beams, 1, step // 2, 2, upchan, samples), lambda i: (i // 2, 0, i % 2, 0, 0, 0, 0)),
        name="filter_power",
    )(matrix, voltages)
    return power.reshape(coarse // 2 * beams, 2, upchan, samples)


def split_of(x):
    high = x.astype(bf16)
    return jnp.concatenate([high, (x - high.astype(f32)).astype(bf16)], axis=1)


def eye_mask(size):
    row = lax.broadcasted_iota(jnp.int32, (size, size), 0)
    return row == lax.broadcasted_iota(jnp.int32, (size, size), 1)


def columns_of(table):
    eye = jnp.where(eye_mask(table.shape[1]), 1.0, 0.0).astype(bf16)
    columns = lax.dot_general(eye, table.astype(bf16), (((1,), (1,)), ((), ())), preferred_element_type=f32)
    return columns.astype(jnp.int32)


def take_rows(split, source):
    trials = split.shape[0]
    samples = split.shape[1] // 2
    lane = lax.broadcasted_iota(jnp.int32, (trials, trials), 1)
    onehot = jnp.where(lane == source, 1.0, 0.0).astype(bf16)
    y = jnp.dot(onehot, split, preferred_element_type=f32)
    return y[:, :samples] + y[:, samples:]


def delay_rows(x, delay):
    trials, samples = x.shape
    half = samples // 2
    lane = lax.broadcasted_iota(jnp.int32, (trials, half), 1)
    index = (lane - delay) & (half - 1)
    inside = lane >= delay
    first = jnp.take_along_axis(x[:, :half], index, axis=1)
    second = jnp.take_along_axis(x[:, half:], index, axis=1)
    return jnp.concatenate([jnp.where(inside, first, 0.0), jnp.where(inside, second, first)], axis=1)


def merge_unit(split_ref, table, level):
    columns = columns_of(table)
    lower = take_rows(split_ref[0], columns[:, 3 * level : 3 * level + 1])
    upper = take_rows(split_ref[1], columns[:, 3 * level + 1 : 3 * level + 2])
    return lower + delay_rows(upper, columns[:, 3 * level + 2 : 3 * level + 3])


STEPS = 65534.0


def put_message(out_ref, x, table):
    trials = x.shape[0]
    peak = jnp.maximum(jnp.max(x, axis=1, keepdims=True), 1e-30)
    code = jnp.floor(jnp.log2(peak) * 256.0) + 2.0
    scale = jnp.exp2(code * (-1.0 / 256.0)) * STEPS
    out_ref[:trials] = ((x * scale + 0.5).astype(jnp.int32) - int(STEPS) // 2).astype(jnp.int16)
    code_row = jnp.sum(jnp.where(eye_mask(trials), code, 0.0), axis=0, keepdims=True).astype(jnp.int32)
    row = lax.broadcasted_iota(jnp.int32, table.shape, 0)
    rows = jnp.where(row == 0, code_row >> 8, jnp.where(row == 1, code_row & 255, table.astype(jnp.int32)))
    out_ref[trials:] = rows.astype(jnp.int16)


def take_message(in_ref, trials):
    table = in_ref[trials:].astype(jnp.int32).astype(f32)
    columns = columns_of(table)
    code = (columns[:, 0:1] * 256 + columns[:, 1:2]).astype(f32)
    scale = jnp.exp2(code * (1.0 / 256.0)) * (1.0 / STEPS)
    x = (in_ref[:trials].astype(jnp.int32) + int(STEPS) // 2).astype(f32) * scale
    return x, table


def dedisperse_kernel(bits_ref, arrived_ref, first_ref, second_ref, sent_ref, split_ref, table_ref, stack_ref):
    sources, _, upchan, samples = arrived_ref.shape
    trials = split_ref.shape[1]
    channels = sources * upchan
    first = bits_ref[BEAM_BIT]
    for in_ref, unit in ((first_ref, first), (second_ref, 1 - first)):
        x = arrived_ref[:, pl.ds(unit, 1)].reshape(channels, samples).astype(f32)
        for inner in range(INNER):
            moved = x if inner == 0 else shifted(x, inner)
            stack_ref[inner * channels : (inner + 1) * channels] = moved.astype(bf16)
        delays = in_ref[:trials]
        total = jnp.zeros((trials, samples), f32)
        for outer in reversed(range(SHIFTS // INNER)):
            onehot = jnp.concatenate(
                [
                    jnp.where(delays == jnp.asarray(outer * INNER + inner, bf16), jnp.asarray(1, bf16), jnp.asarray(0, bf16))
                    for inner in range(INNER)
                ],
                axis=1,
            )
            if outer != SHIFTS // INNER - 1:
                total = shifted(total, INNER)
            total = total + jnp.dot(onehot, stack_ref[...], preferred_element_type=f32)
        split_ref[unit] = split_of(total)
        packed = in_ref[trials:].astype(f32)
        table_ref[unit] = jnp.concatenate([packed[:, :samples], packed[:, samples:]], axis=0)
    put_sent(0, bits_ref, split_ref, table_ref, sent_ref)


def put_sent(level, bits_ref, split_ref, table_ref, sent_ref):
    table = table_ref[1 - bits_ref[SWAP_BITS[level]]]
    put_message(sent_ref, merge_unit(split_ref, table, level), table)


def kept_kernel(level, bits_ref, split_in_ref, table_in_ref, split_ref, table_ref):
    table = table_in_ref[bits_ref[SWAP_BITS[level]]]
    split_ref[...] = split_of(merge_unit(split_in_ref, table, level))
    table_ref[...] = table


def load_units(own, kept_split_ref, kept_table_ref, received_ref, split_ref, table_ref):
    split_ref[own] = kept_split_ref[...]
    table_ref[own] = kept_table_ref[...]
    x, table = take_message(received_ref, kept_split_ref.shape[0])
    split_ref[1 - own] = split_of(x)
    table_ref[1 - own] = table


def sent_kernel(level, bits_ref, kept_split_ref, kept_table_ref, received_ref, sent_ref, split_ref, table_ref):
    load_units(bits_ref[SWAP_BITS[level - 1]], kept_split_ref, kept_table_ref, received_ref, split_ref, table_ref)
    put_sent(level, bits_ref, split_ref, table_ref, sent_ref)


def peaks_kernel(level, bits_ref, kept_split_ref, kept_table_ref, received_ref, first_ref, second_ref, split_ref, table_ref):
    load_units(bits_ref[SWAP_BITS[level - 1]], kept_split_ref, kept_table_ref, received_ref, split_ref, table_ref)
    for out_ref, unit in ((first_ref, bits_ref[BEAM_BIT]), (second_ref, 1 - bits_ref[BEAM_BIT])):
        merged = merge_unit(split_ref, table_ref[unit], level)
        series = merged.T
        samples = series.shape[0]
        mean = jnp.sum(series, axis=0, keepdims=True) * (1.0 / samples)
        centred = series - mean
        variance = jnp.sum(centred * centred, axis=0, keepdims=True) * (1.0 / samples)
        boxcar = centred * lax.rsqrt(variance + epsilon)
        peaks = [jnp.max(boxcar, axis=0, keepdims=True)]
        width = 1
        for _ in range(1, WIDTHS):
            row = lax.broadcasted_iota(jnp.int32, boxcar.shape, 0)
            boxcar = boxcar + jnp.where(row >= width, pltpu.roll(boxcar, width, 0), 0.0)
            width *= 2
            peaks.append(jnp.max(boxcar, axis=0, keepdims=True) * (1.0 / math.sqrt(width)))
        out_ref[...] = jnp.concatenate(peaks, axis=0)


def join_kernel(level, bits_ref, first_ref, second_ref, out_ref):
    out_ref[bits_ref[level]] = first_ref[...]
    out_ref[1 - bits_ref[level]] = second_ref[...]


VMEM = pl.BlockSpec(memory_space=pltpu.VMEM)
SMEM = pl.BlockSpec(memory_space=pltpu.SMEM)


def call(kernel, name, outs, operands, scratch=(), mebibytes=8):
    return pl.pallas_call(
        kernel,
        out_shape=tuple(jax.ShapeDtypeStruct(shape, dtype) for shape, dtype in outs),
        in_specs=[SMEM] + [VMEM] * (len(operands) - 1),
        out_specs=tuple(VMEM for _ in outs),
        scratch_shapes=list(scratch),
        compiler_params=pltpu.CompilerParams(vmem_limit_bytes=mebibytes << 20),
        name=name,
    )(*operands)


def move(x, target):
    return lax.ppermute(x, "freq", [(i, target(i)) for i in range(lax.axis_size("freq"))])


def swap(x, bit):
    return move(x, lambda i: i ^ (1 << bit))


def bit(number, index):
    return number >> index & 1


def gather_units(x):
    def target(flip):
        def device(g):
            low = g >> 1 & (1 << BEAM_BIT) - 1
            return low | (bit(g, 0) ^ flip) << BEAM_BIT | g >> (BEAM_BIT + 1) << (BEAM_BIT + 1)

        return device

    return move(x, target(0)), move(x, target(1))


def home(flip, top):
    def device(d):
        low = d & (1 << BEAM_BIT) - 1
        return low | d >> (BEAM_BIT + 1) << BEAM_BIT | (bit(d, BEAM_BIT) ^ flip) << top

    return device


def local(voltages, sub_delays, merge_tables):
    freq_count = lax.axis_size("freq")
    levels = freq_count.bit_length() - 1
    trials, channels = sub_delays.shape
    samples = voltages.shape[4]
    upchan = voltages.shape[3]
    position = lax.axis_index("freq")
    bits = (position >> jnp.arange(8, dtype=jnp.int32)) & 1

    power = filter_power(voltages)
    arrived = lax.all_to_all(power, "freq", split_axis=0, concat_axis=0, tiled=True)

    rows = -(-3 * levels // 16) * 16
    table = jnp.pad(merge_tables.reshape(3 * levels, trials), ((0, rows - 3 * levels), (0, 0)))
    table = table.reshape(2, rows // 2, trials).transpose(1, 0, 2).reshape(rows // 2, 2 * trials)
    first, second = gather_units(jnp.concatenate([sub_delays, table], axis=0).astype(bf16))

    message = ((trials + rows, samples), jnp.int16)
    splits, both_tables = ((2, trials, 2 * samples), bf16), ((2, rows, samples), f32)
    split, table = ((trials, 2 * samples), bf16), ((rows, samples), f32)
    stack = pltpu.VMEM((INNER * channels, samples), bf16)
    sent, *both = call(
        dedisperse_kernel, "dedisperse", (message, splits, both_tables), (bits, arrived, first, second), [stack], 24
    )
    for level in range(levels - 1):
        received = swap(sent, SWAP_BITS[level])
        kept = call(functools.partial(kept_kernel, level), "kept", (split, table), (bits, *both))
        if level < levels - 2:
            sent, *both = call(
                functools.partial(sent_kernel, level + 1), "sent", (message, splits, both_tables), (bits, *kept, received)
            )
    peak = ((WIDTHS, trials), f32)
    scratch = [pltpu.VMEM(*splits), pltpu.VMEM(*both_tables)]
    first, second = call(
        functools.partial(peaks_kernel, levels - 1), "peaks", (peak, peak), (bits, *kept, received), scratch
    )
    first, second = move(first, home(0, levels - 1)), move(second, home(1, levels - 1))
    return call(
        functools.partial(join_kernel, levels - 1), "join", (((2, WIDTHS, trials), f32),), (bits, first, second)
    )[0]


def solution(mesh):
    return jax.shard_map(
        local,
        mesh=mesh,
        in_specs=(P(None, "beam", "freq", None, None), P("freq", None), P(None, None, "freq")),
        out_specs=P("beam", None, "freq"),
        check_vma=False,
    )
```

```python
import functools
import math

import jax
import jax.numpy as jnp
import numpy as np
from jax import lax
from jax.experimental import pallas as pl
from jax.experimental.pallas import tpu as pltpu
from jax.sharding import PartitionSpec as P

TAPS = 4
WIDTHS = 8
SHIFTS = 32
INNER = 4

BEAM_BIT = 0
SWAP_BITS = (1, 2, 3, 4)

epsilon = 1e-06
f32 = jnp.float32
bf16 = jnp.bfloat16


def filter_matrix(upchan):
    length = TAPS * upchan
    n = np.arange(length, dtype=np.float64)
    window = np.sinc((n - (length - 1) / 2) / upchan) * (0.5 - 0.5 * np.cos(2 * np.pi * (n + 0.5) / length))
    window = (window / np.sqrt(2 * np.sum(window * window))).reshape(TAPS, upchan)
    phase = np.arange(upchan)
    angle = 2 * np.pi * (phase[:, None] * phase[None, :]) / upchan
    cosine, sine = np.cos(angle), np.sin(angle)
    transform = np.block([[cosine, sine], [-sine, cosine]])
    full = np.concatenate([transform * np.tile(window[tap], 2)[None, :] for tap in range(TAPS)], axis=1)
    pieces, rest = [], full
    for _ in range(2):
        piece = rest.astype(jnp.bfloat16)
        pieces.append(piece)
        rest = rest - piece.astype(np.float64)
    return np.concatenate(pieces, axis=0)


def shifted(x, amount):
    lane = lax.broadcasted_iota(jnp.int32, x.shape, 1)
    return jnp.where(lane >= amount, pltpu.roll(x, amount, 1), 0.0)


def filter_kernel(matrix_hbm, volts_hbm, out_hbm, matrix_ref, volts_ref, out_ref, in_sems, out_sems):
    chunks, _, beams, count, upchan, samples = volts_ref.shape
    matrix_copy = pltpu.make_async_copy(matrix_hbm, matrix_ref, in_sems.at[chunks])
    matrix_copy.start()
    loads, stores = [], []
    for chunk in range(chunks):
        source = volts_hbm.at[:, :, pl.ds(chunk * count, count)]
        loads.append(pltpu.make_async_copy(source, volts_ref.at[chunk], in_sems.at[chunk]))
        target = out_hbm.at[pl.ds(chunk * count // 2 * beams, count // 2 * beams)]
        stores.append(pltpu.make_async_copy(out_ref.at[chunk], target, out_sems.at[chunk]))
        loads[chunk].start()
    matrix_copy.wait()
    matrix = matrix_ref[...]
    rows = 2 * upchan
    low = (1 << BEAM_BIT) - 1
    for chunk in range(chunks):
        loads[chunk].wait()
        for q in range(count):
            for beam in range(beams):
                x = volts_ref[chunk, :, beam, q].astype(f32).reshape(rows, samples)
                taps = [x] + [shifted(x, tap) for tap in range(1, TAPS)]
                stacked = jnp.concatenate(taps, axis=0).astype(bf16)
                y = jnp.dot(matrix, stacked, preferred_element_type=f32)
                y = y[:rows] + y[rows:]
                power = y[:upchan] * y[:upchan] + y[upchan:] * y[upchan:]
                half = q // 2
                place = half & low | beam << BEAM_BIT | half >> BEAM_BIT << (BEAM_BIT + 1)
                out_ref[chunk, place, q % 2] = power.astype(bf16)
        stores[chunk].start()
    for store in stores:
        store.wait()


def filter_power(voltages):
    parts, beams, coarse, upchan, samples = voltages.shape
    chunks = 4
    count = coarse // chunks
    matrix = jnp.asarray(filter_matrix(upchan))
    return pl.pallas_call(
        filter_kernel,
        out_shape=jax.ShapeDtypeStruct((coarse // 2 * beams, 2, upchan, samples), bf16),
        in_specs=[pl.BlockSpec(memory_space=pl.ANY), pl.BlockSpec(memory_space=pl.ANY)],
        out_specs=pl.BlockSpec(memory_space=pl.ANY),
        scratch_shapes=[
            pltpu.VMEM(matrix.shape, bf16),
            pltpu.VMEM((chunks, parts, beams, count, upchan, samples), bf16),
            pltpu.VMEM((chunks, count // 2 * beams, 2, upchan, samples), bf16),
            pltpu.SemaphoreType.DMA((chunks + 1,)),
            pltpu.SemaphoreType.DMA((chunks,)),
        ],
        name="filter_power",
    )(matrix, voltages)


def split_of(x):
    high = x.astype(bf16)
    return jnp.concatenate([high, (x - high.astype(f32)).astype(bf16)], axis=1)


def eye_mask(size):
    row = lax.broadcasted_iota(jnp.int32, (size, size), 0)
    return row == lax.broadcasted_iota(jnp.int32, (size, size), 1)


def columns_of(table):
    eye = jnp.where(eye_mask(table.shape[1]), 1.0, 0.0).astype(bf16)
    columns = lax.dot_general(eye, table.astype(bf16), (((1,), (1,)), ((), ())), preferred_element_type=f32)
    return columns.astype(jnp.int32)


def take_rows(split, source):
    trials = split.shape[0]
    samples = split.shape[1] // 2
    lane = lax.broadcasted_iota(jnp.int32, (trials, trials), 1)
    onehot = jnp.where(lane == source, 1.0, 0.0).astype(bf16)
    y = jnp.dot(onehot, split, preferred_element_type=f32)
    return y[:, :samples] + y[:, samples:]


def delay_rows(x, delay):
    trials, samples = x.shape
    half = samples // 2
    lane = lax.broadcasted_iota(jnp.int32, (trials, half), 1)
    index = (lane - delay) & (half - 1)
    inside = lane >= delay
    first = jnp.take_along_axis(x[:, :half], index, axis=1)
    second = jnp.take_along_axis(x[:, half:], index, axis=1)
    return jnp.concatenate([jnp.where(inside, first, 0.0), jnp.where(inside, second, first)], axis=1)


def merge_unit(split_ref, table, level):
    columns = columns_of(table)
    lower = take_rows(split_ref[0], columns[:, 3 * level : 3 * level + 1])
    upper = take_rows(split_ref[1], columns[:, 3 * level + 1 : 3 * level + 2])
    return lower + delay_rows(upper, columns[:, 3 * level + 2 : 3 * level + 3])


STEPS = 65534.0


def put_message(out_ref, x, table):
    trials = x.shape[0]
    peak = jnp.maximum(jnp.max(x, axis=1, keepdims=True), 1e-30)
    code = jnp.floor(jnp.log2(peak) * 256.0) + 2.0
    scale = jnp.exp2(code * (-1.0 / 256.0)) * STEPS
    out_ref[:trials] = ((x * scale + 0.5).astype(jnp.int32) - int(STEPS) // 2).astype(jnp.int16)
    code_row = jnp.sum(jnp.where(eye_mask(trials), code, 0.0), axis=0, keepdims=True).astype(jnp.int32)
    row = lax.broadcasted_iota(jnp.int32, table.shape, 0)
    rows = jnp.where(row == 0, code_row >> 8, jnp.where(row == 1, code_row & 255, table.astype(jnp.int32)))
    out_ref[trials:] = rows.astype(jnp.int16)


def take_message(in_ref, trials):
    table = in_ref[trials:].astype(jnp.int32).astype(f32)
    columns = columns_of(table)
    code = (columns[:, 0:1] * 256 + columns[:, 1:2]).astype(f32)
    scale = jnp.exp2(code * (1.0 / 256.0)) * (1.0 / STEPS)
    x = (in_ref[:trials].astype(jnp.int32) + int(STEPS) // 2).astype(f32) * scale
    return x, table


def dedisperse_kernel(bits_ref, arrived_ref, first_ref, second_ref, sent_ref, split_ref, table_ref, stack_ref):
    sources, _, upchan, samples = arrived_ref.shape
    trials = split_ref.shape[1]
    channels = sources * upchan
    first = bits_ref[BEAM_BIT]
    for in_ref, unit in ((first_ref, first), (second_ref, 1 - first)):
        x = arrived_ref[:, pl.ds(unit, 1)].reshape(channels, samples).astype(f32)
        for inner in range(INNER):
            moved = x if inner == 0 else shifted(x, inner)
            stack_ref[inner * channels : (inner + 1) * channels] = moved.astype(bf16)
        delays = in_ref[:trials]
        total = jnp.zeros((trials, samples), f32)
        for outer in reversed(range(SHIFTS // INNER)):
            onehot = jnp.concatenate(
                [
                    jnp.where(delays == jnp.asarray(outer * INNER + inner, bf16), jnp.asarray(1, bf16), jnp.asarray(0, bf16))
                    for inner in range(INNER)
                ],
                axis=1,
            )
            if outer != SHIFTS // INNER - 1:
                total = shifted(total, INNER)
            total = total + jnp.dot(onehot, stack_ref[...], preferred_element_type=f32)
        split_ref[unit] = split_of(total)
        packed = in_ref[trials:].astype(f32)
        table_ref[unit] = jnp.concatenate([packed[:, :samples], packed[:, samples:]], axis=0)
    put_sent(0, bits_ref, split_ref, table_ref, sent_ref)


def put_sent(level, bits_ref, split_ref, table_ref, sent_ref):
    table = table_ref[1 - bits_ref[SWAP_BITS[level]]]
    put_message(sent_ref, merge_unit(split_ref, table, level), table)


def kept_kernel(level, bits_ref, split_in_ref, table_in_ref, split_ref, table_ref):
    table = table_in_ref[bits_ref[SWAP_BITS[level]]]
    split_ref[...] = split_of(merge_unit(split_in_ref, table, level))
    table_ref[...] = table


def load_units(own, kept_split_ref, kept_table_ref, received_ref, split_ref, table_ref):
    split_ref[own] = kept_split_ref[...]
    table_ref[own] = kept_table_ref[...]
    x, table = take_message(received_ref, kept_split_ref.shape[0])
    split_ref[1 - own] = split_of(x)
    table_ref[1 - own] = table


def sent_kernel(level, bits_ref, kept_split_ref, kept_table_ref, received_ref, sent_ref, split_ref, table_ref):
    load_units(bits_ref[SWAP_BITS[level - 1]], kept_split_ref, kept_table_ref, received_ref, split_ref, table_ref)
    put_sent(level, bits_ref, split_ref, table_ref, sent_ref)


def unit_peaks(merged):
    series = merged.T
    samples = series.shape[0]
    mean = jnp.sum(series, axis=0, keepdims=True) * (1.0 / samples)
    centred = series - mean
    variance = jnp.sum(centred * centred, axis=0, keepdims=True) * (1.0 / samples)
    boxcar = centred * lax.rsqrt(variance + epsilon)
    peaks = [jnp.max(boxcar, axis=0, keepdims=True)]
    width = 1
    for _ in range(1, WIDTHS):
        row = lax.broadcasted_iota(jnp.int32, boxcar.shape, 0)
        boxcar = boxcar + jnp.where(row >= width, pltpu.roll(boxcar, width, 0), 0.0)
        width *= 2
        peaks.append(jnp.max(boxcar, axis=0, keepdims=True) * (1.0 / math.sqrt(width)))
    return jnp.concatenate(peaks, axis=0)


def sent_peaks_kernel(level, bits_ref, kept_split_ref, kept_table_ref, received_ref, peaks_ref, split_ref, table_ref):
    load_units(bits_ref[SWAP_BITS[level - 1]], kept_split_ref, kept_table_ref, received_ref, split_ref, table_ref)
    peaks_ref[...] = unit_peaks(merge_unit(split_ref, table_ref[1 - bits_ref[BEAM_BIT]], level))


def kept_peaks_kernel(level, bits_ref, split_ref, table_ref, peaks_ref):
    peaks_ref[...] = unit_peaks(merge_unit(split_ref, table_ref[bits_ref[BEAM_BIT]], level))


def join_kernel(bits_ref, kept_ref, received_ref, out_ref):
    out_ref[bits_ref[BEAM_BIT]] = kept_ref[...]
    out_ref[1 - bits_ref[BEAM_BIT]] = received_ref[...]


VMEM = pl.BlockSpec(memory_space=pltpu.VMEM)
SMEM = pl.BlockSpec(memory_space=pltpu.SMEM)


def call(kernel, name, outs, operands, scratch=(), mebibytes=8):
    return pl.pallas_call(
        kernel,
        out_shape=tuple(jax.ShapeDtypeStruct(shape, dtype) for shape, dtype in outs),
        in_specs=[SMEM] + [VMEM] * (len(operands) - 1),
        out_specs=tuple(VMEM for _ in outs),
        scratch_shapes=list(scratch),
        compiler_params=pltpu.CompilerParams(vmem_limit_bytes=mebibytes << 20),
        name=name,
    )(*operands)


def move(x, target):
    pairs = [(i, target(i)) for i in range(lax.axis_size("freq"))]
    return x if all(i == j for i, j in pairs) else lax.ppermute(x, "freq", pairs)


def swap(x, bit):
    return move(x, lambda i: i ^ (1 << bit))


def bit(number, index):
    return number >> index & 1


def gather_units(x):
    def target(flip):
        def device(g):
            low = g >> 1 & (1 << BEAM_BIT) - 1
            return low | (bit(g, 0) ^ flip) << BEAM_BIT | g >> (BEAM_BIT + 1) << (BEAM_BIT + 1)

        return device

    return move(x, target(0)), move(x, target(1))


def home(top):
    def device(d):
        low = d & (1 << BEAM_BIT) - 1
        return low | d >> (BEAM_BIT + 1) << BEAM_BIT | bit(d, BEAM_BIT) << top

    return device


def local(voltages, sub_delays, merge_tables):
    freq_count = lax.axis_size("freq")
    levels = freq_count.bit_length() - 1
    trials, channels = sub_delays.shape
    samples = voltages.shape[4]
    upchan = voltages.shape[3]
    position = lax.axis_index("freq")
    bits = (position >> jnp.arange(8, dtype=jnp.int32)) & 1

    power = filter_power(voltages)
    arrived = lax.all_to_all(power, "freq", split_axis=0, concat_axis=0, tiled=True)

    rows = -(-3 * levels // 16) * 16
    table = jnp.pad(merge_tables.reshape(3 * levels, trials), ((0, rows - 3 * levels), (0, 0)))
    table = table.reshape(2, rows // 2, trials).transpose(1, 0, 2).reshape(rows // 2, 2 * trials)
    first, second = gather_units(jnp.concatenate([sub_delays, table], axis=0).astype(bf16))

    message = ((trials + rows, samples), jnp.int16)
    splits, both_tables = ((2, trials, 2 * samples), bf16), ((2, rows, samples), f32)
    split, table = ((trials, 2 * samples), bf16), ((rows, samples), f32)
    stack = pltpu.VMEM((INNER * channels, samples), bf16)
    sent, *both = call(
        dedisperse_kernel, "dedisperse", (message, splits, both_tables), (bits, arrived, first, second), [stack], 24
    )
    for level in range(levels - 1):
        received = swap(sent, SWAP_BITS[level])
        kept = call(functools.partial(kept_kernel, level), "kept", (split, table), (bits, *both))
        if level < levels - 2:
            sent, *both = call(
                functools.partial(sent_kernel, level + 1), "sent", (message, splits, both_tables), (bits, *kept, received)
            )
    peak = ((WIDTHS, trials), f32)
    sent, *both = call(
        functools.partial(sent_peaks_kernel, levels - 1), "sent_peaks", (peak, splits, both_tables), (bits, *kept, received)
    )
    received = swap(sent, BEAM_BIT)
    kept = call(functools.partial(kept_peaks_kernel, levels - 1), "kept_peaks", (peak,), (bits, *both))
    peaks = call(join_kernel, "join", (((2, WIDTHS, trials), f32),), (bits, *kept, received))[0]
    return move(peaks, home(levels - 1))


def solution(mesh):
    return jax.shard_map(
        local,
        mesh=mesh,
        in_specs=(P(None, "beam", "freq", None, None), P("freq", None), P(None, None, "freq")),
        out_specs=P("beam", None, "freq"),
        check_vma=False,
    )
```

```python
import functools
import math

import jax
import jax.numpy as jnp
import numpy as np
from jax import lax
from jax.experimental import pallas as pl
from jax.experimental.pallas import tpu as pltpu
from jax.sharding import PartitionSpec as P

TAPS = 4
WIDTHS = 8
SHIFTS = 32
INNER = 4

BEAM_BIT = 0
PARTNERS = (2, 6, 8, 24)


def bit(number, index):
    return number >> index & 1


KEEPS = (
    lambda d: bit(d, 1) ^ bit(d, 2),
    lambda d: 1 - bit(d, 1),
    lambda d: bit(d, 3) ^ bit(d, 4),
    lambda d: 1 - bit(d, 3),
    lambda d: bit(d, 0),
)


def home(d):
    return sum(keep(d) << level for level, keep in enumerate(KEEPS))


epsilon = 1e-06
f32 = jnp.float32
bf16 = jnp.bfloat16


def filter_matrix(upchan):
    length = TAPS * upchan
    n = np.arange(length, dtype=np.float64)
    window = np.sinc((n - (length - 1) / 2) / upchan) * (0.5 - 0.5 * np.cos(2 * np.pi * (n + 0.5) / length))
    window = (window / np.sqrt(2 * np.sum(window * window))).reshape(TAPS, upchan)
    phase = np.arange(upchan)
    angle = 2 * np.pi * (phase[:, None] * phase[None, :]) / upchan
    cosine, sine = np.cos(angle), np.sin(angle)
    transform = np.block([[cosine, sine], [-sine, cosine]])
    full = np.concatenate([transform * np.tile(window[tap], 2)[None, :] for tap in range(TAPS)], axis=1)
    pieces, rest = [], full
    for _ in range(2):
        piece = rest.astype(jnp.bfloat16)
        pieces.append(piece)
        rest = rest - piece.astype(np.float64)
    return np.concatenate(pieces, axis=0)


def shifted(x, amount):
    lane = lax.broadcasted_iota(jnp.int32, x.shape, 1)
    return jnp.where(lane >= amount, pltpu.roll(x, amount, 1), 0.0)


def filter_kernel(matrix_hbm, volts_hbm, out_hbm, matrix_ref, volts_ref, out_ref, in_sems, out_sems):
    chunks, _, beams, count, upchan, samples = volts_ref.shape
    matrix_copy = pltpu.make_async_copy(matrix_hbm, matrix_ref, in_sems.at[chunks])
    matrix_copy.start()
    loads, stores = [], []
    for chunk in range(chunks):
        source = volts_hbm.at[:, :, pl.ds(chunk * count, count)]
        loads.append(pltpu.make_async_copy(source, volts_ref.at[chunk], in_sems.at[chunk]))
        target = out_hbm.at[pl.ds(chunk * count // 2 * beams, count // 2 * beams)]
        stores.append(pltpu.make_async_copy(out_ref.at[chunk], target, out_sems.at[chunk]))
        loads[chunk].start()
    matrix_copy.wait()
    matrix = matrix_ref[...]
    rows = 2 * upchan
    low = (1 << BEAM_BIT) - 1
    for chunk in range(chunks):
        loads[chunk].wait()
        for q in range(count):
            for beam in range(beams):
                x = volts_ref[chunk, :, beam, q].astype(f32).reshape(rows, samples)
                taps = [x] + [shifted(x, tap) for tap in range(1, TAPS)]
                stacked = jnp.concatenate(taps, axis=0).astype(bf16)
                y = jnp.dot(matrix, stacked, preferred_element_type=f32)
                y = y[:rows] + y[rows:]
                power = y[:upchan] * y[:upchan] + y[upchan:] * y[upchan:]
                half = q // 2
                place = half & low | beam << BEAM_BIT | half >> BEAM_BIT << (BEAM_BIT + 1)
                out_ref[chunk, place, q % 2] = power.astype(bf16)
        stores[chunk].start()
    for store in stores:
        store.wait()


def filter_power(voltages):
    parts, beams, coarse, upchan, samples = voltages.shape
    chunks = 4
    count = coarse // chunks
    matrix = jnp.asarray(filter_matrix(upchan))
    return pl.pallas_call(
        filter_kernel,
        out_shape=jax.ShapeDtypeStruct((coarse // 2 * beams, 2, upchan, samples), bf16),
        in_specs=[pl.BlockSpec(memory_space=pl.ANY), pl.BlockSpec(memory_space=pl.ANY)],
        out_specs=pl.BlockSpec(memory_space=pl.ANY),
        scratch_shapes=[
            pltpu.VMEM(matrix.shape, bf16),
            pltpu.VMEM((chunks, parts, beams, count, upchan, samples), bf16),
            pltpu.VMEM((chunks, count // 2 * beams, 2, upchan, samples), bf16),
            pltpu.SemaphoreType.DMA((chunks + 1,)),
            pltpu.SemaphoreType.DMA((chunks,)),
        ],
        name="filter_power",
    )(matrix, voltages)


def split_of(x):
    high = x.astype(bf16)
    return jnp.concatenate([high, (x - high.astype(f32)).astype(bf16)], axis=1)


def eye_mask(size):
    row = lax.broadcasted_iota(jnp.int32, (size, size), 0)
    return row == lax.broadcasted_iota(jnp.int32, (size, size), 1)


def columns_of(table):
    eye = jnp.where(eye_mask(table.shape[1]), 1.0, 0.0).astype(bf16)
    columns = lax.dot_general(eye, table.astype(bf16), (((1,), (1,)), ((), ())), preferred_element_type=f32)
    return columns.astype(jnp.int32)


def take_rows(split, source):
    trials = split.shape[0]
    samples = split.shape[1] // 2
    lane = lax.broadcasted_iota(jnp.int32, (trials, trials), 1)
    onehot = jnp.where(lane == source, 1.0, 0.0).astype(bf16)
    y = jnp.dot(onehot, split, preferred_element_type=f32)
    return y[:, :samples] + y[:, samples:]


def delay_rows(x, delay):
    trials, samples = x.shape
    half = samples // 2
    lane = lax.broadcasted_iota(jnp.int32, (trials, half), 1)
    index = (lane - delay) & (half - 1)
    inside = lane >= delay
    first = jnp.take_along_axis(x[:, :half], index, axis=1)
    second = jnp.take_along_axis(x[:, half:], index, axis=1)
    return jnp.concatenate([jnp.where(inside, first, 0.0), jnp.where(inside, second, first)], axis=1)


def merge_unit(split_ref, table, level):
    columns = columns_of(table)
    lower = take_rows(split_ref[0], columns[:, 3 * level : 3 * level + 1])
    upper = take_rows(split_ref[1], columns[:, 3 * level + 1 : 3 * level + 2])
    return lower + delay_rows(upper, columns[:, 3 * level + 2 : 3 * level + 3])


STEPS = 65534.0

KEEP = 5


def put_message(out_ref, x, table):
    trials = x.shape[0]
    peak = jnp.maximum(jnp.max(x, axis=1, keepdims=True), 1e-30)
    code = jnp.floor(jnp.log2(peak) * 256.0) + 2.0
    scale = jnp.exp2(code * (-1.0 / 256.0)) * STEPS
    out_ref[:trials] = ((x * scale + 0.5).astype(jnp.int32) - int(STEPS) // 2).astype(jnp.int16)
    code_row = jnp.sum(jnp.where(eye_mask(trials), code, 0.0), axis=0, keepdims=True).astype(jnp.int32)
    row = lax.broadcasted_iota(jnp.int32, table.shape, 0)
    rows = jnp.where(row == 0, code_row >> 8, jnp.where(row == 1, code_row & 255, table.astype(jnp.int32)))
    out_ref[trials:] = rows.astype(jnp.int16)


def take_message(in_ref, trials):
    table = in_ref[trials:].astype(jnp.int32).astype(f32)
    columns = columns_of(table)
    code = (columns[:, 0:1] * 256 + columns[:, 1:2]).astype(f32)
    scale = jnp.exp2(code * (1.0 / 256.0)) * (1.0 / STEPS)
    x = (in_ref[:trials].astype(jnp.int32) + int(STEPS) // 2).astype(f32) * scale
    return x, table


def dedisperse_kernel(bits_ref, arrived_ref, first_ref, second_ref, sent_ref, split_ref, table_ref, stack_ref):
    sources, _, upchan, samples = arrived_ref.shape
    trials = split_ref.shape[1]
    channels = sources * upchan
    first = bits_ref[0]
    for in_ref, unit in ((first_ref, first), (second_ref, 1 - first)):
        x = arrived_ref[:, pl.ds(unit, 1)].reshape(channels, samples).astype(f32)
        for inner in range(INNER):
            moved = x if inner == 0 else shifted(x, inner)
            stack_ref[inner * channels : (inner + 1) * channels] = moved.astype(bf16)
        delays = in_ref[:trials]
        total = jnp.zeros((trials, samples), f32)
        for outer in reversed(range(SHIFTS // INNER)):
            onehot = jnp.concatenate(
                [
                    jnp.where(delays == jnp.asarray(outer * INNER + inner, bf16), jnp.asarray(1, bf16), jnp.asarray(0, bf16))
                    for inner in range(INNER)
                ],
                axis=1,
            )
            if outer != SHIFTS // INNER - 1:
                total = shifted(total, INNER)
            total = total + jnp.dot(onehot, stack_ref[...], preferred_element_type=f32)
        split_ref[unit] = split_of(total)
        packed = in_ref[trials:].astype(f32)
        table_ref[unit] = jnp.concatenate([packed[:, :samples], packed[:, samples:]], axis=0)
    put_sent(0, bits_ref, split_ref, table_ref, sent_ref)


def put_sent(level, bits_ref, split_ref, table_ref, sent_ref):
    table = table_ref[1 - bits_ref[KEEP + level]]
    put_message(sent_ref, merge_unit(split_ref, table, level), table)


def kept_kernel(level, bits_ref, split_in_ref, table_in_ref, split_ref, table_ref):
    table = table_in_ref[bits_ref[KEEP + level]]
    split_ref[...] = split_of(merge_unit(split_in_ref, table, level))
    table_ref[...] = table


def load_units(own, kept_split_ref, kept_table_ref, received_ref, split_ref, table_ref):
    split_ref[own] = kept_split_ref[...]
    table_ref[own] = kept_table_ref[...]
    x, table = take_message(received_ref, kept_split_ref.shape[0])
    split_ref[1 - own] = split_of(x)
    table_ref[1 - own] = table


def sent_kernel(level, bits_ref, kept_split_ref, kept_table_ref, received_ref, sent_ref, split_ref, table_ref):
    load_units(bits_ref[level], kept_split_ref, kept_table_ref, received_ref, split_ref, table_ref)
    put_sent(level, bits_ref, split_ref, table_ref, sent_ref)


def unit_peaks(merged):
    series = merged.T
    samples = series.shape[0]
    mean = jnp.sum(series, axis=0, keepdims=True) * (1.0 / samples)
    centred = series - mean
    variance = jnp.sum(centred * centred, axis=0, keepdims=True) * (1.0 / samples)
    boxcar = centred * lax.rsqrt(variance + epsilon)
    peaks = [jnp.max(boxcar, axis=0, keepdims=True)]
    width = 1
    for _ in range(1, WIDTHS):
        row = lax.broadcasted_iota(jnp.int32, boxcar.shape, 0)
        boxcar = boxcar + jnp.where(row >= width, pltpu.roll(boxcar, width, 0), 0.0)
        width *= 2
        peaks.append(jnp.max(boxcar, axis=0, keepdims=True) * (1.0 / math.sqrt(width)))
    return jnp.concatenate(peaks, axis=0)


def sent_peaks_kernel(level, bits_ref, kept_split_ref, kept_table_ref, received_ref, peaks_ref, split_ref, table_ref):
    load_units(bits_ref[level], kept_split_ref, kept_table_ref, received_ref, split_ref, table_ref)
    peaks_ref[...] = unit_peaks(merge_unit(split_ref, table_ref[1 - bits_ref[KEEP + level]], level))


def kept_peaks_kernel(level, bits_ref, split_ref, table_ref, peaks_ref):
    peaks_ref[...] = unit_peaks(merge_unit(split_ref, table_ref[bits_ref[KEEP + level]], level))


def join_kernel(bits_ref, kept_ref, received_ref, out_ref):
    out_ref[bits_ref[0]] = kept_ref[...]
    out_ref[1 - bits_ref[0]] = received_ref[...]


VMEM = pl.BlockSpec(memory_space=pltpu.VMEM)
SMEM = pl.BlockSpec(memory_space=pltpu.SMEM)


def call(kernel, name, outs, operands, scratch=(), mebibytes=8):
    return pl.pallas_call(
        kernel,
        out_shape=tuple(jax.ShapeDtypeStruct(shape, dtype) for shape, dtype in outs),
        in_specs=[SMEM] + [VMEM] * (len(operands) - 1),
        out_specs=tuple(VMEM for _ in outs),
        scratch_shapes=list(scratch),
        compiler_params=pltpu.CompilerParams(vmem_limit_bytes=mebibytes << 20),
        name=name,
    )(*operands)


def move(x, target):
    pairs = [(i, target(i)) for i in range(lax.axis_size("freq"))]
    return x if all(i == j for i, j in pairs) else lax.ppermute(x, "freq", pairs)


def swap(x, mask):
    return move(x, lambda i: i ^ mask)


def gather_units(x):
    def target(flip):
        def device(g):
            low = g >> 1 & (1 << BEAM_BIT) - 1
            return low | (bit(g, 0) ^ flip) << BEAM_BIT | g >> (BEAM_BIT + 1) << (BEAM_BIT + 1)

        return device

    return move(x, target(0)), move(x, target(1))


def local(voltages, sub_delays, merge_tables):
    freq_count = lax.axis_size("freq")
    levels = freq_count.bit_length() - 1
    trials, channels = sub_delays.shape
    samples = voltages.shape[4]
    upchan = voltages.shape[3]
    position = lax.axis_index("freq")
    bits = [bit(position, index) for index in range(levels)] + [keep(position) for keep in KEEPS]
    bits = jnp.stack(bits + [0] * (16 - len(bits))).astype(jnp.int32)

    power = filter_power(voltages)
    arrived = lax.all_to_all(power, "freq", split_axis=0, concat_axis=0, tiled=True)

    rows = -(-3 * levels // 16) * 16
    table = jnp.pad(merge_tables.reshape(3 * levels, trials), ((0, rows - 3 * levels), (0, 0)))
    table = table.reshape(2, rows // 2, trials).transpose(1, 0, 2).reshape(rows // 2, 2 * trials)
    first, second = gather_units(jnp.concatenate([sub_delays, table], axis=0).astype(bf16))

    message = ((trials + rows, samples), jnp.int16)
    splits, both_tables = ((2, trials, 2 * samples), bf16), ((2, rows, samples), f32)
    split, table = ((trials, 2 * samples), bf16), ((rows, samples), f32)
    stack = pltpu.VMEM((INNER * channels, samples), bf16)
    sent, *both = call(
        dedisperse_kernel, "dedisperse", (message, splits, both_tables), (bits, arrived, first, second), [stack], 24
    )
    for level in range(levels - 1):
        received = swap(sent, PARTNERS[level])
        kept = call(functools.partial(kept_kernel, level), "kept", (split, table), (bits, *both))
        if level < levels - 2:
            sent, *both = call(
                functools.partial(sent_kernel, level + 1), "sent", (message, splits, both_tables), (bits, *kept, received)
            )
    peak = ((WIDTHS, trials), f32)
    sent, *both = call(
        functools.partial(sent_peaks_kernel, levels - 1), "sent_peaks", (peak, splits, both_tables), (bits, *kept, received)
    )
    received = swap(sent, 1 << BEAM_BIT)
    kept = call(functools.partial(kept_peaks_kernel, levels - 1), "kept_peaks", (peak,), (bits, *both))
    peaks = call(join_kernel, "join", (((2, WIDTHS, trials), f32),), (bits, *kept, received))[0]
    return move(peaks, home)


def solution(mesh):
    return jax.shard_map(
        local,
        mesh=mesh,
        in_specs=(P(None, "beam", "freq", None, None), P("freq", None), P(None, None, "freq")),
        out_specs=P("beam", None, "freq"),
        check_vma=False,
    )
```

```python
import functools
import math

import jax
import jax.numpy as jnp
import numpy as np
from jax import lax
from jax.experimental import pallas as pl
from jax.experimental.pallas import tpu as pltpu
from jax.sharding import PartitionSpec as P

TAPS = 4
WIDTHS = 8
SHIFTS = 32
INNER = 4

BEAM_BIT = 0
PARTNERS = (2, 6, 8, 24)


def bit(number, index):
    return number >> index & 1


KEEPS = (
    lambda d: bit(d, 1) ^ bit(d, 2),
    lambda d: 1 - bit(d, 1),
    lambda d: bit(d, 3) ^ bit(d, 4),
    lambda d: 1 - bit(d, 3),
    lambda d: bit(d, 0),
)


def here():
    return lax.axis_index("freq")


def home(d):
    return sum(keep(d) << level for level, keep in enumerate(KEEPS))


epsilon = 1e-06
f32 = jnp.float32
bf16 = jnp.bfloat16


def filter_matrix(upchan):
    length = TAPS * upchan
    n = np.arange(length, dtype=np.float64)
    window = np.sinc((n - (length - 1) / 2) / upchan) * (0.5 - 0.5 * np.cos(2 * np.pi * (n + 0.5) / length))
    window = (window / np.sqrt(2 * np.sum(window * window))).reshape(TAPS, upchan)
    phase = np.arange(upchan)
    angle = 2 * np.pi * (phase[:, None] * phase[None, :]) / upchan
    cosine, sine = np.cos(angle), np.sin(angle)
    transform = np.block([[cosine, sine], [-sine, cosine]])
    full = np.concatenate([transform * np.tile(window[tap], 2)[None, :] for tap in range(TAPS)], axis=1)
    pieces, rest = [], full
    for _ in range(2):
        piece = rest.astype(jnp.bfloat16)
        pieces.append(piece)
        rest = rest - piece.astype(np.float64)
    return np.concatenate(pieces, axis=0)


def shifted(x, amount):
    lane = lax.broadcasted_iota(jnp.int32, x.shape, 1)
    return jnp.where(lane >= amount, pltpu.roll(x, amount, 1), 0.0)


def filter_kernel(matrix_hbm, volts_hbm, out_hbm, matrix_ref, volts_ref, out_ref, in_sems, out_sems):
    chunks, _, beams, count, upchan, samples = volts_ref.shape
    matrix_copy = pltpu.make_async_copy(matrix_hbm, matrix_ref, in_sems.at[chunks])
    matrix_copy.start()
    loads, stores = [], []
    for chunk in range(chunks):
        source = volts_hbm.at[:, :, pl.ds(chunk * count, count)]
        loads.append(pltpu.make_async_copy(source, volts_ref.at[chunk], in_sems.at[chunk]))
        target = out_hbm.at[pl.ds(chunk * count // 2 * beams, count // 2 * beams)]
        stores.append(pltpu.make_async_copy(out_ref.at[chunk], target, out_sems.at[chunk]))
        loads[chunk].start()
    matrix_copy.wait()
    matrix = matrix_ref[...]
    rows = 2 * upchan
    low = (1 << BEAM_BIT) - 1
    for chunk in range(chunks):
        loads[chunk].wait()
        for q in range(count):
            for beam in range(beams):
                x = volts_ref[chunk, :, beam, q].astype(f32).reshape(rows, samples)
                taps = [x] + [shifted(x, tap) for tap in range(1, TAPS)]
                stacked = jnp.concatenate(taps, axis=0).astype(bf16)
                y = jnp.dot(matrix, stacked, preferred_element_type=f32)
                y = y[:rows] + y[rows:]
                power = y[:upchan] * y[:upchan] + y[upchan:] * y[upchan:]
                half = q // 2
                place = half & low | beam << BEAM_BIT | half >> BEAM_BIT << (BEAM_BIT + 1)
                out_ref[chunk, place, q % 2] = power.astype(bf16)
        stores[chunk].start()
    for store in stores:
        store.wait()


def filter_power(voltages):
    parts, beams, coarse, upchan, samples = voltages.shape
    chunks = 4
    count = coarse // chunks
    matrix = jnp.asarray(filter_matrix(upchan))
    return pl.pallas_call(
        filter_kernel,
        out_shape=jax.ShapeDtypeStruct((coarse // 2 * beams, 2, upchan, samples), bf16),
        in_specs=[pl.BlockSpec(memory_space=pl.ANY), pl.BlockSpec(memory_space=pl.ANY)],
        out_specs=pl.BlockSpec(memory_space=pl.ANY),
        scratch_shapes=[
            pltpu.VMEM(matrix.shape, bf16),
            pltpu.VMEM((chunks, parts, beams, count, upchan, samples), bf16),
            pltpu.VMEM((chunks, count // 2 * beams, 2, upchan, samples), bf16),
            pltpu.SemaphoreType.DMA((chunks + 1,)),
            pltpu.SemaphoreType.DMA((chunks,)),
        ],
        name="filter_power",
    )(matrix, voltages)


def split_of(x):
    high = x.astype(bf16)
    return jnp.concatenate([high, (x - high.astype(f32)).astype(bf16)], axis=1)


def eye_mask(size):
    row = lax.broadcasted_iota(jnp.int32, (size, size), 0)
    return row == lax.broadcasted_iota(jnp.int32, (size, size), 1)


def columns_of(table):
    eye = jnp.where(eye_mask(table.shape[1]), 1.0, 0.0).astype(bf16)
    columns = lax.dot_general(eye, table.astype(bf16), (((1,), (1,)), ((), ())), preferred_element_type=f32)
    return columns.astype(jnp.int32)


def take_rows(split, source):
    trials = split.shape[0]
    samples = split.shape[1] // 2
    lane = lax.broadcasted_iota(jnp.int32, (trials, trials), 1)
    onehot = jnp.where(lane == source, 1.0, 0.0).astype(bf16)
    y = jnp.dot(onehot, split, preferred_element_type=f32)
    return y[:, :samples] + y[:, samples:]


def delay_rows(x, delay):
    trials, samples = x.shape
    half = samples // 2
    lane = lax.broadcasted_iota(jnp.int32, (trials, half), 1)
    index = (lane - delay) & (half - 1)
    inside = lane >= delay
    first = jnp.take_along_axis(x[:, :half], index, axis=1)
    second = jnp.take_along_axis(x[:, half:], index, axis=1)
    return jnp.concatenate([jnp.where(inside, first, 0.0), jnp.where(inside, second, first)], axis=1)


def merge_unit(split_ref, table, level):
    columns = columns_of(table)
    lower = take_rows(split_ref[0], columns[:, 3 * level : 3 * level + 1])
    upper = take_rows(split_ref[1], columns[:, 3 * level + 1 : 3 * level + 2])
    return lower + delay_rows(upper, columns[:, 3 * level + 2 : 3 * level + 3])


STEPS = 65534.0


def put_message(out_ref, x, table):
    trials = x.shape[0]
    peak = jnp.maximum(jnp.max(x, axis=1, keepdims=True), 1e-30)
    code = jnp.floor(jnp.log2(peak) * 256.0) + 2.0
    scale = jnp.exp2(code * (-1.0 / 256.0)) * STEPS
    out_ref[:trials] = ((x * scale + 0.5).astype(jnp.int32) - int(STEPS) // 2).astype(jnp.int16)
    code_row = jnp.sum(jnp.where(eye_mask(trials), code, 0.0), axis=0, keepdims=True).astype(jnp.int32)
    row = lax.broadcasted_iota(jnp.int32, table.shape, 0)
    rows = jnp.where(row == 0, code_row >> 8, jnp.where(row == 1, code_row & 255, table.astype(jnp.int32)))
    out_ref[trials:] = rows.astype(jnp.int16)


def take_message(in_ref, trials):
    table = in_ref[trials:].astype(jnp.int32).astype(f32)
    columns = columns_of(table)
    code = (columns[:, 0:1] * 256 + columns[:, 1:2]).astype(f32)
    scale = jnp.exp2(code * (1.0 / 256.0)) * (1.0 / STEPS)
    x = (in_ref[:trials].astype(jnp.int32) + int(STEPS) // 2).astype(f32) * scale
    return x, table


def dedisperse_kernel(arrived_ref, first_ref, second_ref, sent_ref, split_ref, table_ref, stack_ref):
    sources, _, upchan, samples = arrived_ref.shape
    trials = split_ref.shape[1]
    channels = sources * upchan
    first = bit(here(), BEAM_BIT)
    for in_ref, unit in ((first_ref, first), (second_ref, 1 - first)):
        x = arrived_ref[:, pl.ds(unit, 1)].reshape(channels, samples).astype(f32)
        for inner in range(INNER):
            moved = x if inner == 0 else shifted(x, inner)
            stack_ref[inner * channels : (inner + 1) * channels] = moved.astype(bf16)
        delays = in_ref[:trials]
        total = jnp.zeros((trials, samples), f32)
        for outer in reversed(range(SHIFTS // INNER)):
            onehot = jnp.concatenate(
                [
                    jnp.where(delays == jnp.asarray(outer * INNER + inner, bf16), jnp.asarray(1, bf16), jnp.asarray(0, bf16))
                    for inner in range(INNER)
                ],
                axis=1,
            )
            if outer != SHIFTS // INNER - 1:
                total = shifted(total, INNER)
            total = total + jnp.dot(onehot, stack_ref[...], preferred_element_type=f32)
        split_ref[unit] = split_of(total)
        packed = in_ref[trials:].astype(f32)
        table_ref[unit] = jnp.concatenate([packed[:, :samples], packed[:, samples:]], axis=0)
    put_sent(0, split_ref, table_ref, sent_ref)


def put_sent(level, split_ref, table_ref, sent_ref):
    table = table_ref[1 - KEEPS[level](here())]
    put_message(sent_ref, merge_unit(split_ref, table, level), table)


def kept_kernel(level, split_in_ref, table_in_ref, split_ref, table_ref):
    table = table_in_ref[KEEPS[level](here())]
    split_ref[...] = split_of(merge_unit(split_in_ref, table, level))
    table_ref[...] = table


def load_units(own, kept_split_ref, kept_table_ref, received_ref, split_ref, table_ref):
    split_ref[own] = kept_split_ref[...]
    table_ref[own] = kept_table_ref[...]
    x, table = take_message(received_ref, kept_split_ref.shape[0])
    split_ref[1 - own] = split_of(x)
    table_ref[1 - own] = table


def sent_kernel(level, kept_split_ref, kept_table_ref, received_ref, sent_ref, split_ref, table_ref):
    load_units(bit(here(), level), kept_split_ref, kept_table_ref, received_ref, split_ref, table_ref)
    put_sent(level, split_ref, table_ref, sent_ref)


def unit_peaks(merged):
    series = merged.T
    samples = series.shape[0]
    mean = jnp.sum(series, axis=0, keepdims=True) * (1.0 / samples)
    centred = series - mean
    variance = jnp.sum(centred * centred, axis=0, keepdims=True) * (1.0 / samples)
    boxcar = centred * lax.rsqrt(variance + epsilon)
    peaks = [jnp.max(boxcar, axis=0, keepdims=True)]
    width = 1
    for _ in range(1, WIDTHS):
        row = lax.broadcasted_iota(jnp.int32, boxcar.shape, 0)
        boxcar = boxcar + jnp.where(row >= width, pltpu.roll(boxcar, width, 0), 0.0)
        width *= 2
        peaks.append(jnp.max(boxcar, axis=0, keepdims=True) * (1.0 / math.sqrt(width)))
    return jnp.concatenate(peaks, axis=0)


def sent_peaks_kernel(level, kept_split_ref, kept_table_ref, received_ref, peaks_ref, split_ref, table_ref):
    load_units(bit(here(), level), kept_split_ref, kept_table_ref, received_ref, split_ref, table_ref)
    peaks_ref[...] = unit_peaks(merge_unit(split_ref, table_ref[1 - KEEPS[level](here())], level))


def kept_peaks_kernel(level, split_ref, table_ref, peaks_ref):
    peaks_ref[...] = unit_peaks(merge_unit(split_ref, table_ref[KEEPS[level](here())], level))


def join_kernel(kept_ref, received_ref, out_ref):
    beam = bit(here(), BEAM_BIT)
    out_ref[beam] = kept_ref[...]
    out_ref[1 - beam] = received_ref[...]


VMEM = pl.BlockSpec(memory_space=pltpu.VMEM)


def call(kernel, name, outs, operands, scratch=(), mebibytes=8):
    return pl.pallas_call(
        kernel,
        out_shape=tuple(jax.ShapeDtypeStruct(shape, dtype) for shape, dtype in outs),
        in_specs=[VMEM] * len(operands),
        out_specs=tuple(VMEM for _ in outs),
        scratch_shapes=list(scratch),
        compiler_params=pltpu.CompilerParams(vmem_limit_bytes=mebibytes << 20),
        name=name,
    )(*operands)


def move(x, target):
    pairs = [(i, target(i)) for i in range(lax.axis_size("freq"))]
    return x if all(i == j for i, j in pairs) else lax.ppermute(x, "freq", pairs)


def swap(x, mask):
    return move(x, lambda i: i ^ mask)


def gather_units(x):
    def target(flip):
        def device(g):
            low = g >> 1 & (1 << BEAM_BIT) - 1
            return low | (bit(g, 0) ^ flip) << BEAM_BIT | g >> (BEAM_BIT + 1) << (BEAM_BIT + 1)

        return device

    return move(x, target(0)), move(x, target(1))


def local(voltages, sub_delays, merge_tables):
    freq_count = lax.axis_size("freq")
    levels = freq_count.bit_length() - 1
    trials, channels = sub_delays.shape
    samples = voltages.shape[4]
    upchan = voltages.shape[3]
    power = filter_power(voltages)
    arrived = lax.all_to_all(power, "freq", split_axis=0, concat_axis=0, tiled=True)

    rows = -(-3 * levels // 16) * 16
    table = jnp.pad(merge_tables.reshape(3 * levels, trials), ((0, rows - 3 * levels), (0, 0)))
    table = table.reshape(2, rows // 2, trials).transpose(1, 0, 2).reshape(rows // 2, 2 * trials)
    first, second = gather_units(jnp.concatenate([sub_delays, table], axis=0).astype(bf16))

    message = ((trials + rows, samples), jnp.int16)
    splits, both_tables = ((2, trials, 2 * samples), bf16), ((2, rows, samples), f32)
    split, table = ((trials, 2 * samples), bf16), ((rows, samples), f32)
    stack = pltpu.VMEM((INNER * channels, samples), bf16)
    sent, *both = call(
        dedisperse_kernel, "dedisperse", (message, splits, both_tables), (arrived, first, second), [stack], 24
    )
    for level in range(levels - 1):
        received = swap(sent, PARTNERS[level])
        kept = call(functools.partial(kept_kernel, level), "kept", (split, table), tuple(both))
        if level < levels - 2:
            sent, *both = call(
                functools.partial(sent_kernel, level + 1), "sent", (message, splits, both_tables), (*kept, received)
            )
    peak = ((WIDTHS, trials), f32)
    sent, *both = call(
        functools.partial(sent_peaks_kernel, levels - 1), "sent_peaks", (peak, splits, both_tables), (*kept, received)
    )
    received = swap(sent, 1 << BEAM_BIT)
    kept = call(functools.partial(kept_peaks_kernel, levels - 1), "kept_peaks", (peak,), tuple(both))
    peaks = call(join_kernel, "join", (((2, WIDTHS, trials), f32),), (*kept, received))[0]
    return move(peaks, home)


def solution(mesh):
    return jax.shard_map(
        local,
        mesh=mesh,
        in_specs=(P(None, "beam", "freq", None, None), P("freq", None), P(None, None, "freq")),
        out_specs=P("beam", None, "freq"),
        check_vma=False,
    )
```

```python
import functools
import math

import jax
import jax.numpy as jnp
import numpy as np
from jax import lax
from jax.experimental import pallas as pl
from jax.experimental.pallas import tpu as pltpu
from jax.sharding import PartitionSpec as P

TAPS = 4
WIDTHS = 8
SHIFTS = 32
INNER = 4

BEAM_BIT = 0
PARTNERS = (2, 6, 8, 24)


def bit(number, index):
    return number >> index & 1


KEEPS = (
    lambda d: bit(d, 1) ^ bit(d, 2),
    lambda d: 1 - bit(d, 1),
    lambda d: bit(d, 3) ^ bit(d, 4),
    lambda d: 1 - bit(d, 3),
    lambda d: bit(d, 0),
)


def here():
    return lax.axis_index("freq")


def home(d):
    return sum(keep(d) << level for level, keep in enumerate(KEEPS))


epsilon = 1e-06
f32 = jnp.float32
bf16 = jnp.bfloat16


def filter_matrix(upchan):
    length = TAPS * upchan
    n = np.arange(length, dtype=np.float64)
    window = np.sinc((n - (length - 1) / 2) / upchan) * (0.5 - 0.5 * np.cos(2 * np.pi * (n + 0.5) / length))
    window = (window / np.sqrt(2 * np.sum(window * window))).reshape(TAPS, upchan)
    phase = np.arange(upchan)
    angle = 2 * np.pi * (phase[:, None] * phase[None, :]) / upchan
    cosine, sine = np.cos(angle), np.sin(angle)
    transform = np.block([[cosine, sine], [-sine, cosine]])
    full = np.concatenate([transform * np.tile(window[tap], 2)[None, :] for tap in range(TAPS)], axis=1)
    pieces, rest = [], full
    for _ in range(2):
        piece = rest.astype(jnp.bfloat16)
        pieces.append(piece)
        rest = rest - piece.astype(np.float64)
    return np.concatenate(pieces, axis=0)


def shifted(x, amount):
    rolled = pltpu.roll(x, amount, 1)
    head = rolled[:, :128]
    lane = lax.broadcasted_iota(jnp.int32, head.shape, 1)
    return jnp.concatenate([jnp.where(lane >= amount, head, 0.0), rolled[:, 128:]], axis=1)


def filter_kernel(matrix_hbm, volts_hbm, out_hbm, matrix_ref, volts_ref, out_ref, in_sems, out_sems):
    chunks, _, beams, count, upchan, samples = volts_ref.shape
    matrix_copy = pltpu.make_async_copy(matrix_hbm, matrix_ref, in_sems.at[chunks])
    matrix_copy.start()
    loads, stores = [], []
    for chunk in range(chunks):
        source = volts_hbm.at[:, :, pl.ds(chunk * count, count)]
        loads.append(pltpu.make_async_copy(source, volts_ref.at[chunk], in_sems.at[chunk]))
        target = out_hbm.at[pl.ds(chunk * count // 2 * beams, count // 2 * beams)]
        stores.append(pltpu.make_async_copy(out_ref.at[chunk], target, out_sems.at[chunk]))
        loads[chunk].start()
    matrix_copy.wait()
    matrix = matrix_ref[...]
    rows = 2 * upchan
    low = (1 << BEAM_BIT) - 1
    for chunk in range(chunks):
        loads[chunk].wait()
        for q in range(count):
            for beam in range(beams):
                x = volts_ref[chunk, :, beam, q].astype(f32).reshape(rows, samples)
                taps = [x] + [shifted(x, tap) for tap in range(1, TAPS)]
                stacked = jnp.concatenate(taps, axis=0).astype(bf16)
                y = jnp.dot(matrix, stacked, preferred_element_type=f32)
                y = y[:rows] + y[rows:]
                power = y[:upchan] * y[:upchan] + y[upchan:] * y[upchan:]
                half = q // 2
                place = half & low | beam << BEAM_BIT | half >> BEAM_BIT << (BEAM_BIT + 1)
                out_ref[chunk, place, q % 2] = power.astype(bf16)
        stores[chunk].start()
    for store in stores:
        store.wait()


def filter_power(voltages):
    parts, beams, coarse, upchan, samples = voltages.shape
    chunks = 2
    count = coarse // chunks
    matrix = jnp.asarray(filter_matrix(upchan))
    return pl.pallas_call(
        filter_kernel,
        out_shape=jax.ShapeDtypeStruct((coarse // 2 * beams, 2, upchan, samples), bf16),
        in_specs=[pl.BlockSpec(memory_space=pl.ANY), pl.BlockSpec(memory_space=pl.ANY)],
        out_specs=pl.BlockSpec(memory_space=pl.ANY),
        scratch_shapes=[
            pltpu.VMEM(matrix.shape, bf16),
            pltpu.VMEM((chunks, parts, beams, count, upchan, samples), bf16),
            pltpu.VMEM((chunks, count // 2 * beams, 2, upchan, samples), bf16),
            pltpu.SemaphoreType.DMA((chunks + 1,)),
            pltpu.SemaphoreType.DMA((chunks,)),
        ],
        name="filter_power",
    )(matrix, voltages)


def split_of(x):
    high = x.astype(bf16)
    return jnp.concatenate([high, (x - high.astype(f32)).astype(bf16)], axis=1)


def eye_mask(size):
    row = lax.broadcasted_iota(jnp.int32, (size, size), 0)
    return row == lax.broadcasted_iota(jnp.int32, (size, size), 1)


def columns_of(table):
    eye = jnp.where(eye_mask(table.shape[1]), 1.0, 0.0).astype(bf16)
    columns = lax.dot_general(eye, table.astype(bf16), (((1,), (1,)), ((), ())), preferred_element_type=f32)
    return columns.astype(jnp.int32)


def take_rows(split, source):
    trials = split.shape[0]
    samples = split.shape[1] // 2
    lane = lax.broadcasted_iota(jnp.int32, (trials, trials), 1)
    onehot = jnp.where(lane == source, 1.0, 0.0).astype(bf16)
    y = jnp.dot(onehot, split, preferred_element_type=f32)
    return y[:, :samples] + y[:, samples:]


def delay_rows(x, delay):
    trials, samples = x.shape
    half = samples // 2
    lane = lax.broadcasted_iota(jnp.int32, (trials, half), 1)
    index = (lane - delay) & (half - 1)
    inside = lane >= delay
    first = jnp.take_along_axis(x[:, :half], index, axis=1)
    second = jnp.take_along_axis(x[:, half:], index, axis=1)
    return jnp.concatenate([jnp.where(inside, first, 0.0), jnp.where(inside, second, first)], axis=1)


def merge_unit(split_ref, table, level):
    columns = columns_of(table)
    lower = take_rows(split_ref[0], columns[:, 3 * level : 3 * level + 1])
    upper = take_rows(split_ref[1], columns[:, 3 * level + 1 : 3 * level + 2])
    return lower + delay_rows(upper, columns[:, 3 * level + 2 : 3 * level + 3])


STEPS = 65534.0


def put_message(out_ref, x, table):
    trials = x.shape[0]
    peak = jnp.maximum(jnp.max(x, axis=1, keepdims=True), 1e-30)
    code = jnp.floor(jnp.log2(peak) * 256.0) + 2.0
    scale = jnp.exp2(code * (-1.0 / 256.0)) * STEPS
    out_ref[:trials] = ((x * scale + 0.5).astype(jnp.int32) - int(STEPS) // 2).astype(jnp.int16)
    code_row = jnp.sum(jnp.where(eye_mask(trials), code, 0.0), axis=0, keepdims=True).astype(jnp.int32)
    row = lax.broadcasted_iota(jnp.int32, table.shape, 0)
    rows = jnp.where(row == 0, code_row >> 8, jnp.where(row == 1, code_row & 255, table.astype(jnp.int32)))
    out_ref[trials:] = rows.astype(jnp.int16)


def take_message(in_ref, trials):
    table = in_ref[trials:].astype(jnp.int32).astype(f32)
    columns = columns_of(table)
    code = (columns[:, 0:1] * 256 + columns[:, 1:2]).astype(f32)
    scale = jnp.exp2(code * (1.0 / 256.0)) * (1.0 / STEPS)
    x = (in_ref[:trials].astype(jnp.int32) + int(STEPS) // 2).astype(f32) * scale
    return x, table


def dedisperse_kernel(arrived_ref, tables_ref, sent_ref, split_ref, table_ref, stack_ref):
    sources, _, upchan, samples = arrived_ref.shape
    trials = split_ref.shape[1]
    channels = sources * upchan
    for unit in range(2):
        x = arrived_ref[:, unit].reshape(channels, samples).astype(f32)
        for inner in range(INNER):
            moved = x if inner == 0 else shifted(x, inner)
            stack_ref[inner * channels : (inner + 1) * channels] = moved.astype(bf16)
        delays = tables_ref[unit, :trials]
        total = jnp.zeros((trials, samples), f32)
        for outer in reversed(range(SHIFTS // INNER)):
            onehot = jnp.concatenate(
                [
                    jnp.where(delays == jnp.asarray(outer * INNER + inner, bf16), jnp.asarray(1, bf16), jnp.asarray(0, bf16))
                    for inner in range(INNER)
                ],
                axis=1,
            )
            if outer != SHIFTS // INNER - 1:
                total = shifted(total, INNER)
            total = total + jnp.dot(onehot, stack_ref[...], preferred_element_type=f32)
        split_ref[unit] = split_of(total)
        packed = tables_ref[unit, trials:].astype(f32)
        table_ref[unit] = jnp.concatenate([packed[:, :samples], packed[:, samples:]], axis=0)
    put_sent(0, split_ref, table_ref, sent_ref)


def put_sent(level, split_ref, table_ref, sent_ref):
    table = table_ref[1 - KEEPS[level](here())]
    put_message(sent_ref, merge_unit(split_ref, table, level), table)


def kept_kernel(level, split_in_ref, table_in_ref, split_ref, table_ref):
    table = table_in_ref[KEEPS[level](here())]
    split_ref[...] = split_of(merge_unit(split_in_ref, table, level))
    table_ref[...] = table


def load_units(own, kept_split_ref, kept_table_ref, received_ref, split_ref, table_ref):
    split_ref[own] = kept_split_ref[...]
    table_ref[own] = kept_table_ref[...]
    x, table = take_message(received_ref, kept_split_ref.shape[0])
    split_ref[1 - own] = split_of(x)
    table_ref[1 - own] = table


def sent_kernel(level, kept_split_ref, kept_table_ref, received_ref, sent_ref, split_ref, table_ref):
    load_units(bit(here(), level), kept_split_ref, kept_table_ref, received_ref, split_ref, table_ref)
    put_sent(level, split_ref, table_ref, sent_ref)


def unit_peaks(merged):
    series = merged.T
    samples = series.shape[0]
    mean = jnp.sum(series, axis=0, keepdims=True) * (1.0 / samples)
    centred = series - mean
    variance = jnp.sum(centred * centred, axis=0, keepdims=True) * (1.0 / samples)
    boxcar = centred * lax.rsqrt(variance + epsilon)
    peaks = [jnp.max(boxcar, axis=0, keepdims=True)]
    width = 1
    for _ in range(1, WIDTHS):
        row = lax.broadcasted_iota(jnp.int32, boxcar.shape, 0)
        boxcar = boxcar + jnp.where(row >= width, pltpu.roll(boxcar, width, 0), 0.0)
        width *= 2
        peaks.append(jnp.max(boxcar, axis=0, keepdims=True) * (1.0 / math.sqrt(width)))
    return jnp.concatenate(peaks, axis=0)


def sent_peaks_kernel(level, kept_split_ref, kept_table_ref, received_ref, peaks_ref, split_ref, table_ref):
    load_units(bit(here(), level), kept_split_ref, kept_table_ref, received_ref, split_ref, table_ref)
    peaks_ref[...] = unit_peaks(merge_unit(split_ref, table_ref[1 - KEEPS[level](here())], level))


def kept_peaks_kernel(level, split_ref, table_ref, peaks_ref):
    peaks_ref[...] = unit_peaks(merge_unit(split_ref, table_ref[KEEPS[level](here())], level))


def join_kernel(kept_ref, received_ref, out_ref):
    beam = bit(here(), BEAM_BIT)
    out_ref[beam] = kept_ref[...]
    out_ref[1 - beam] = received_ref[...]


VMEM = pl.BlockSpec(memory_space=pltpu.VMEM)


def call(kernel, name, outs, operands, scratch=(), mebibytes=8):
    return pl.pallas_call(
        kernel,
        out_shape=tuple(jax.ShapeDtypeStruct(shape, dtype) for shape, dtype in outs),
        in_specs=[VMEM] * len(operands),
        out_specs=tuple(VMEM for _ in outs),
        scratch_shapes=list(scratch),
        compiler_params=pltpu.CompilerParams(vmem_limit_bytes=mebibytes << 20),
        name=name,
    )(*operands)


def move(x, target):
    pairs = [(i, target(i)) for i in range(lax.axis_size("freq"))]
    return x if all(i == j for i, j in pairs) else lax.ppermute(x, "freq", pairs)


def swap(x, mask):
    return move(x, lambda i: i ^ mask)


def gather_units(x):
    def target(flip):
        def device(g):
            low = g >> 1 & (1 << BEAM_BIT) - 1
            return low | (bit(g, 0) ^ flip) << BEAM_BIT | g >> (BEAM_BIT + 1) << (BEAM_BIT + 1)

        return device

    return move(x, target(0)), move(x, target(1))


def local(voltages, sub_delays, merge_tables):
    freq_count = lax.axis_size("freq")
    levels = freq_count.bit_length() - 1
    trials, channels = sub_delays.shape
    samples = voltages.shape[4]
    upchan = voltages.shape[3]
    power = filter_power(voltages)
    arrived = lax.all_to_all(power, "freq", split_axis=0, concat_axis=0, tiled=True)

    rows = -(-3 * levels // 16) * 16
    table = jnp.pad(merge_tables.reshape(3 * levels, trials), ((0, rows - 3 * levels), (0, 0)))
    table = table.reshape(2, rows // 2, trials).transpose(1, 0, 2).reshape(rows // 2, 2 * trials)
    first, second = gather_units(jnp.concatenate([sub_delays, table], axis=0).astype(bf16))
    swapped = bit(here(), BEAM_BIT) == 1
    tables = jnp.stack([jnp.where(swapped, second, first), jnp.where(swapped, first, second)])

    message = ((trials + rows, samples), jnp.int16)
    splits, both_tables = ((2, trials, 2 * samples), bf16), ((2, rows, samples), f32)
    split, table = ((trials, 2 * samples), bf16), ((rows, samples), f32)
    stack = pltpu.VMEM((INNER * channels, samples), bf16)
    sent, *both = call(
        dedisperse_kernel, "dedisperse", (message, splits, both_tables), (arrived, tables), [stack], 24
    )
    for level in range(levels - 1):
        received = swap(sent, PARTNERS[level])
        kept = call(functools.partial(kept_kernel, level), "kept", (split, table), tuple(both))
        if level < levels - 2:
            sent, *both = call(
                functools.partial(sent_kernel, level + 1), "sent", (message, splits, both_tables), (*kept, received)
            )
    peak = ((WIDTHS, trials), f32)
    sent, *both = call(
        functools.partial(sent_peaks_kernel, levels - 1), "sent_peaks", (peak, splits, both_tables), (*kept, received)
    )
    received = swap(sent, 1 << BEAM_BIT)
    kept = call(functools.partial(kept_peaks_kernel, levels - 1), "kept_peaks", (peak,), tuple(both))
    peaks = call(join_kernel, "join", (((2, WIDTHS, trials), f32),), (*kept, received))[0]
    return move(peaks, home)


def solution(mesh):
    return jax.shard_map(
        local,
        mesh=mesh,
        in_specs=(P(None, "beam", "freq", None, None), P("freq", None), P(None, None, "freq")),
        out_specs=P("beam", None, "freq"),
        check_vma=False,
    )
```

```python
import functools
import math

import jax
import jax.numpy as jnp
import numpy as np
from jax import lax
from jax.experimental import pallas as pl
from jax.experimental.pallas import tpu as pltpu
from jax.sharding import PartitionSpec as P

TAPS = 4
WIDTHS = 8
SHIFTS = 32
INNER = 4

BEAM_BIT = 0
PARTNERS = (2, 6, 8, 24)


def bit(number, index):
    return number >> index & 1


KEEPS = (
    lambda d: bit(d, 1) ^ bit(d, 2),
    lambda d: 1 - bit(d, 1),
    lambda d: bit(d, 3) ^ bit(d, 4),
    lambda d: 1 - bit(d, 3),
    lambda d: bit(d, 0),
)


def here():
    return lax.axis_index("freq")


def home(d):
    return sum(keep(d) << level for level, keep in enumerate(KEEPS))


epsilon = 1e-06
f32 = jnp.float32
bf16 = jnp.bfloat16


def filter_matrix(upchan):
    length = TAPS * upchan
    n = np.arange(length, dtype=np.float64)
    window = np.sinc((n - (length - 1) / 2) / upchan) * (0.5 - 0.5 * np.cos(2 * np.pi * (n + 0.5) / length))
    window = (window / np.sqrt(2 * np.sum(window * window))).reshape(TAPS, upchan)
    phase = np.arange(upchan)
    angle = 2 * np.pi * (phase[:, None] * phase[None, :]) / upchan
    cosine, sine = np.cos(angle), np.sin(angle)
    transform = np.block([[cosine, sine], [-sine, cosine]])
    full = np.concatenate([transform * np.tile(window[tap], 2)[None, :] for tap in range(TAPS)], axis=1)
    pieces, rest = [], full
    for _ in range(2):
        piece = rest.astype(jnp.bfloat16)
        pieces.append(piece)
        rest = rest - piece.astype(np.float64)
    return np.concatenate(pieces, axis=0)


def shifted(x, amount):
    rolled = pltpu.roll(x, amount, 1)
    head = rolled[:, :128]
    lane = lax.broadcasted_iota(jnp.int32, head.shape, 1)
    return jnp.concatenate([jnp.where(lane >= amount, head, 0.0), rolled[:, 128:]], axis=1)


def filter_kernel(matrix_hbm, volts_hbm, out_hbm, matrix_ref, volts_ref, out_ref, in_sems, out_sems):
    chunks, _, beams, count, upchan, samples = volts_ref.shape
    matrix_copy = pltpu.make_async_copy(matrix_hbm, matrix_ref, in_sems.at[chunks])
    matrix_copy.start()
    loads, stores = [], []
    for chunk in range(chunks):
        source = volts_hbm.at[:, :, pl.ds(chunk * count, count)]
        loads.append(pltpu.make_async_copy(source, volts_ref.at[chunk], in_sems.at[chunk]))
        target = out_hbm.at[pl.ds(chunk * count // 2 * beams, count // 2 * beams)]
        stores.append(pltpu.make_async_copy(out_ref.at[chunk], target, out_sems.at[chunk]))
        loads[chunk].start()
    matrix_copy.wait()
    matrix = matrix_ref[...]
    rows = 2 * upchan
    low = (1 << BEAM_BIT) - 1
    for chunk in range(chunks):
        loads[chunk].wait()
        for q in range(count):
            for beam in range(beams):
                x = volts_ref[chunk, :, beam, q].astype(f32).reshape(rows, samples)
                taps = [x] + [shifted(x, tap) for tap in range(1, TAPS)]
                stacked = jnp.concatenate(taps, axis=0).astype(bf16)
                y = jnp.dot(matrix, stacked, preferred_element_type=f32)
                y = y[:rows] + y[rows:]
                power = y[:upchan] * y[:upchan] + y[upchan:] * y[upchan:]
                half = q // 2
                place = half & low | beam << BEAM_BIT | half >> BEAM_BIT << (BEAM_BIT + 1)
                out_ref[chunk, place, q % 2] = power.astype(bf16)
        stores[chunk].start()
    for store in stores:
        store.wait()


def filter_power(voltages):
    parts, beams, coarse, upchan, samples = voltages.shape
    chunks = 2
    count = coarse // chunks
    matrix = jnp.asarray(filter_matrix(upchan))
    return pl.pallas_call(
        filter_kernel,
        out_shape=jax.ShapeDtypeStruct((coarse // 2 * beams, 2, upchan, samples), bf16),
        in_specs=[pl.BlockSpec(memory_space=pl.ANY), pl.BlockSpec(memory_space=pl.ANY)],
        out_specs=pl.BlockSpec(memory_space=pl.ANY),
        scratch_shapes=[
            pltpu.VMEM(matrix.shape, bf16),
            pltpu.VMEM((chunks, parts, beams, count, upchan, samples), bf16),
            pltpu.VMEM((chunks, count // 2 * beams, 2, upchan, samples), bf16),
            pltpu.SemaphoreType.DMA((chunks + 1,)),
            pltpu.SemaphoreType.DMA((chunks,)),
        ],
        name="filter_power",
    )(matrix, voltages)


def split_of(x):
    high = x.astype(bf16)
    return jnp.concatenate([high, (x - high.astype(f32)).astype(bf16)], axis=0)


def eye_mask(size):
    row = lax.broadcasted_iota(jnp.int32, (size, size), 0)
    return row == lax.broadcasted_iota(jnp.int32, (size, size), 1)


def columns_of(table):
    eye = jnp.where(eye_mask(table.shape[1]), 1.0, 0.0).astype(bf16)
    columns = lax.dot_general(eye, table.astype(bf16), (((1,), (1,)), ((), ())), preferred_element_type=f32)
    return columns.astype(jnp.int32)


def take_rows(split, weight, source):
    trials = weight.shape[1]
    lane = lax.broadcasted_iota(jnp.int32, (trials, trials), 1)
    picked = jnp.where(lane == source, weight, 0.0).astype(bf16)
    return jnp.dot(jnp.concatenate([picked, picked], axis=1), split, preferred_element_type=f32)


def delay_rows(x, delay):
    trials, samples = x.shape
    half = samples // 2
    lane = lax.broadcasted_iota(jnp.int32, (trials, half), 1)
    index = (lane - delay) & (half - 1)
    inside = lane >= delay
    first = jnp.take_along_axis(x[:, :half], index, axis=1)
    second = jnp.take_along_axis(x[:, half:], index, axis=1)
    return jnp.concatenate([jnp.where(inside, first, 0.0), jnp.where(inside, second, first)], axis=1)


def table_row(level):
    return 3 * (len(KEEPS) - 1 - level)


def table_rows(level):
    return -(-(3 * (len(KEEPS) - level) + 2) // 8) * 8


def merge_unit(split_ref, weight_ref, table, level):
    columns = columns_of(table)
    row = table_row(level)
    lower = take_rows(split_ref[0], weight_ref[0], columns[:, row : row + 1])
    upper = take_rows(split_ref[1], weight_ref[1], columns[:, row + 1 : row + 2])
    return lower + delay_rows(upper, columns[:, row + 2 : row + 3])


def scale_of(code):
    return jnp.exp2(code * (1.0 / 256.0)).astype(bf16).astype(f32)


def put_message(out_ref, x, table):
    trials = x.shape[0]
    rows = out_ref.shape[0] - trials
    peak = jnp.maximum(jnp.max(x, axis=1, keepdims=True), 1e-30)
    code = jnp.floor(jnp.log2(peak) * 256.0) + 3.0
    out_ref[:trials] = ((x * (65536.0 / scale_of(code)) + 0.5).astype(jnp.int32) - 32768).astype(jnp.int16)
    code_row = jnp.sum(jnp.where(eye_mask(trials), code, 0.0), axis=0, keepdims=True).astype(jnp.int32)
    table = table[:rows].astype(jnp.int32)
    row = lax.broadcasted_iota(jnp.int32, table.shape, 0)
    filled = jnp.where(row == rows - 2, code_row >> 8, jnp.where(row == rows - 1, code_row & 255, table))
    out_ref[trials:] = filled.astype(jnp.int16)


def take_message(in_ref, trials):
    table = in_ref[trials:].astype(jnp.int32).astype(f32)
    rows = table.shape[0]
    weight = scale_of(table[rows - 2 : rows - 1] * 256.0 + table[rows - 1 :]) * (1.0 / 65536.0)
    x = in_ref[:trials].astype(jnp.int32) + 32768
    split = jnp.concatenate([(x & 0xFF00).astype(f32).astype(bf16), (x & 0xFF).astype(f32).astype(bf16)], axis=0)
    return split, weight, table


def dedisperse_kernel(arrived_ref, tables_ref, sent_ref, split_ref, weight_ref, table_ref, stack_ref):
    sources, _, upchan, samples = arrived_ref.shape
    trials = weight_ref.shape[2]
    weight_ref[...] = jnp.ones(weight_ref.shape, f32)
    channels = sources * upchan
    for unit in range(2):
        x = arrived_ref[:, unit].reshape(channels, samples).astype(f32)
        for inner in range(INNER):
            moved = x if inner == 0 else shifted(x, inner)
            stack_ref[inner * channels : (inner + 1) * channels] = moved.astype(bf16)
        delays = tables_ref[unit, :trials]
        total = jnp.zeros((trials, samples), f32)
        for outer in reversed(range(SHIFTS // INNER)):
            onehot = jnp.concatenate(
                [
                    jnp.where(delays == jnp.asarray(outer * INNER + inner, bf16), jnp.asarray(1, bf16), jnp.asarray(0, bf16))
                    for inner in range(INNER)
                ],
                axis=1,
            )
            if outer != SHIFTS // INNER - 1:
                total = shifted(total, INNER)
            total = total + jnp.dot(onehot, stack_ref[...], preferred_element_type=f32)
        split_ref[unit] = split_of(total)
        packed = tables_ref[unit, trials:].astype(f32)
        table_ref[unit] = jnp.concatenate([packed[:, :samples], packed[:, samples:]], axis=0)
    put_sent(0, split_ref, weight_ref, table_ref, sent_ref)


def put_sent(level, split_ref, weight_ref, table_ref, sent_ref):
    table = table_ref[1 - KEEPS[level](here())]
    put_message(sent_ref, merge_unit(split_ref, weight_ref, table, level), table)


def kept_kernel(level, split_in_ref, weight_in_ref, table_in_ref, split_ref, table_ref):
    table = table_in_ref[KEEPS[level](here())]
    split_ref[...] = split_of(merge_unit(split_in_ref, weight_in_ref, table, level))
    table_ref[...] = table[: table_ref.shape[0]]


def load_units(own, kept_split_ref, kept_table_ref, received_ref, split_ref, weight_ref, table_ref):
    split_ref[own] = kept_split_ref[...]
    weight_ref[own] = jnp.ones(weight_ref.shape[1:], f32)
    table_ref[own] = kept_table_ref[...]
    split, weight, table = take_message(received_ref, weight_ref.shape[2])
    split_ref[1 - own] = split
    weight_ref[1 - own] = weight
    table_ref[1 - own] = table


def sent_kernel(level, kept_split_ref, kept_table_ref, received_ref, sent_ref, split_ref, weight_ref, table_ref):
    own = bit(here(), level)
    load_units(own, kept_split_ref, kept_table_ref, received_ref, split_ref, weight_ref, table_ref)
    put_sent(level, split_ref, weight_ref, table_ref, sent_ref)


def unit_peaks(merged):
    series = merged.T
    samples = series.shape[0]
    mean = jnp.sum(series, axis=0, keepdims=True) * (1.0 / samples)
    centred = series - mean
    variance = jnp.sum(centred * centred, axis=0, keepdims=True) * (1.0 / samples)
    boxcar = centred * lax.rsqrt(variance + epsilon)
    peaks = [jnp.max(boxcar, axis=0, keepdims=True)]
    width = 1
    for _ in range(1, WIDTHS):
        row = lax.broadcasted_iota(jnp.int32, boxcar.shape, 0)
        boxcar = boxcar + jnp.where(row >= width, pltpu.roll(boxcar, width, 0), 0.0)
        width *= 2
        peaks.append(jnp.max(boxcar, axis=0, keepdims=True) * (1.0 / math.sqrt(width)))
    return jnp.concatenate(peaks, axis=0)


def sent_peaks_kernel(level, kept_split_ref, kept_table_ref, received_ref, peaks_ref, split_ref, weight_ref, table_ref):
    own = bit(here(), level)
    load_units(own, kept_split_ref, kept_table_ref, received_ref, split_ref, weight_ref, table_ref)
    peaks_ref[...] = unit_peaks(merge_unit(split_ref, weight_ref, table_ref[1 - KEEPS[level](here())], level))


def kept_peaks_kernel(level, split_ref, weight_ref, table_ref, peaks_ref):
    peaks_ref[...] = unit_peaks(merge_unit(split_ref, weight_ref, table_ref[KEEPS[level](here())], level))


def join_kernel(kept_ref, received_ref, out_ref):
    beam = bit(here(), BEAM_BIT)
    out_ref[beam] = kept_ref[...]
    out_ref[1 - beam] = received_ref[...]


VMEM = pl.BlockSpec(memory_space=pltpu.VMEM)


def call(kernel, name, outs, operands, scratch=(), mebibytes=8):
    return pl.pallas_call(
        kernel,
        out_shape=tuple(jax.ShapeDtypeStruct(shape, dtype) for shape, dtype in outs),
        in_specs=[VMEM] * len(operands),
        out_specs=tuple(VMEM for _ in outs),
        scratch_shapes=list(scratch),
        compiler_params=pltpu.CompilerParams(vmem_limit_bytes=mebibytes << 20),
        name=name,
    )(*operands)


def move(x, target):
    pairs = [(i, target(i)) for i in range(lax.axis_size("freq"))]
    return x if all(i == j for i, j in pairs) else lax.ppermute(x, "freq", pairs)


def swap(x, mask):
    return move(x, lambda i: i ^ mask)


def gather_units(x):
    def target(flip):
        def device(g):
            low = g >> 1 & (1 << BEAM_BIT) - 1
            return low | (bit(g, 0) ^ flip) << BEAM_BIT | g >> (BEAM_BIT + 1) << (BEAM_BIT + 1)

        return device

    return move(x, target(0)), move(x, target(1))


def local(voltages, sub_delays, merge_tables):
    freq_count = lax.axis_size("freq")
    levels = freq_count.bit_length() - 1
    trials, channels = sub_delays.shape
    samples = voltages.shape[4]
    upchan = voltages.shape[3]
    power = filter_power(voltages)
    arrived = lax.all_to_all(power, "freq", split_axis=0, concat_axis=0, tiled=True)

    rows = table_rows(0) // 16 * 16
    table = jnp.pad(merge_tables[::-1].reshape(3 * levels, trials), ((0, rows - 3 * levels), (0, 0)))
    table = table.reshape(2, rows // 2, trials).transpose(1, 0, 2).reshape(rows // 2, 2 * trials)
    first, second = gather_units(jnp.concatenate([sub_delays, table], axis=0).astype(bf16))
    swapped = bit(here(), BEAM_BIT) == 1
    tables = jnp.stack([jnp.where(swapped, second, first), jnp.where(swapped, first, second)])

    def message(level):
        return (trials + table_rows(level), samples), jnp.int16

    def both_units(rows):
        return ((2, 2 * trials, samples), bf16), ((2, 1, trials), f32), ((2, rows, samples), f32)

    stack = pltpu.VMEM((INNER * channels, samples), bf16)
    sent, *both = call(dedisperse_kernel, "dedisperse", (message(1), *both_units(rows)), (arrived, tables), [stack], 24)
    for level in range(1, levels):
        rows = table_rows(level)
        received = swap(sent, PARTNERS[level - 1])
        units = ((2 * trials, samples), bf16), ((rows, samples), f32)
        kept = call(functools.partial(kept_kernel, level - 1), "kept", units, tuple(both))
        last = level == levels - 1
        kernel, name = (sent_peaks_kernel, "sent_peaks") if last else (sent_kernel, "sent")
        out = ((WIDTHS, trials), f32) if last else message(level + 1)
        sent, *both = call(functools.partial(kernel, level), name, (out, *both_units(rows)), (*kept, received))
    received = swap(sent, 1 << BEAM_BIT)
    kept = call(functools.partial(kept_peaks_kernel, levels - 1), "kept_peaks", (out,), tuple(both))
    peaks = call(join_kernel, "join", (((2, WIDTHS, trials), f32),), (*kept, received))[0]
    return move(peaks, home)


def solution(mesh):
    return jax.shard_map(
        local,
        mesh=mesh,
        in_specs=(P(None, "beam", "freq", None, None), P("freq", None), P(None, None, "freq")),
        out_specs=P("beam", None, "freq"),
        check_vma=False,
    )
```

```python
import functools
import math

import jax
import jax.numpy as jnp
import numpy as np
from jax import lax
from jax.experimental import pallas as pl
from jax.experimental.pallas import tpu as pltpu
from jax.sharding import PartitionSpec as P

TAPS = 4
WIDTHS = 8
SHIFTS = 32
INNER = 4

BEAM_BIT = 0
PARTNERS = (2, 6, 8, 24)


def bit(number, index):
    return number >> index & 1


KEEPS = (
    lambda d: bit(d, 1) ^ bit(d, 2),
    lambda d: 1 - bit(d, 1),
    lambda d: bit(d, 3) ^ bit(d, 4),
    lambda d: 1 - bit(d, 3),
    lambda d: bit(d, 0),
)


def here():
    return lax.axis_index("freq")


def home(d):
    return sum(keep(d) << level for level, keep in enumerate(KEEPS))


epsilon = 1e-06
f32 = jnp.float32
bf16 = jnp.bfloat16


def filter_matrix(upchan):
    length = TAPS * upchan
    n = np.arange(length, dtype=np.float64)
    window = np.sinc((n - (length - 1) / 2) / upchan) * (0.5 - 0.5 * np.cos(2 * np.pi * (n + 0.5) / length))
    window = (window / np.sqrt(2 * np.sum(window * window))).reshape(TAPS, upchan)
    phase = np.arange(upchan)
    angle = 2 * np.pi * (phase[:, None] * phase[None, :]) / upchan
    cosine, sine = np.cos(angle), np.sin(angle)
    transform = np.block([[cosine, sine], [-sine, cosine]])
    full = np.concatenate([transform * np.tile(window[tap], 2)[None, :] for tap in range(TAPS)], axis=1)
    pieces, rest = [], full
    for _ in range(2):
        piece = rest.astype(jnp.bfloat16)
        pieces.append(piece)
        rest = rest - piece.astype(np.float64)
    return np.concatenate(pieces, axis=0)


def shifted(x, amount):
    rolled = pltpu.roll(x, amount, 1)
    head = rolled[:, :128]
    lane = lax.broadcasted_iota(jnp.int32, head.shape, 1)
    return jnp.concatenate([jnp.where(lane >= amount, head, 0.0), rolled[:, 128:]], axis=1)


def filter_kernel(matrix_hbm, volts_hbm, out_hbm, matrix_ref, volts_ref, out_ref, in_sems, out_sems):
    chunks, _, beams, count, upchan, samples = volts_ref.shape
    matrix_copy = pltpu.make_async_copy(matrix_hbm, matrix_ref, in_sems.at[chunks])
    matrix_copy.start()
    loads, stores = [], []
    for chunk in range(chunks):
        source = volts_hbm.at[:, :, pl.ds(chunk * count, count)]
        loads.append(pltpu.make_async_copy(source, volts_ref.at[chunk], in_sems.at[chunk]))
        target = out_hbm.at[pl.ds(chunk * count // 2 * beams, count // 2 * beams)]
        stores.append(pltpu.make_async_copy(out_ref.at[chunk], target, out_sems.at[chunk]))
        loads[chunk].start()
    matrix_copy.wait()
    matrix = matrix_ref[...]
    rows = 2 * upchan
    low = (1 << BEAM_BIT) - 1
    for chunk in range(chunks):
        loads[chunk].wait()
        for q in range(count):
            for beam in range(beams):
                x = volts_ref[chunk, :, beam, q].astype(f32).reshape(rows, samples)
                taps = [x] + [shifted(x, tap) for tap in range(1, TAPS)]
                stacked = jnp.concatenate(taps, axis=0).astype(bf16)
                y = jnp.dot(matrix, stacked, preferred_element_type=f32)
                y = y[:rows] + y[rows:]
                power = y[:upchan] * y[:upchan] + y[upchan:] * y[upchan:]
                half = q // 2
                place = half & low | beam << BEAM_BIT | half >> BEAM_BIT << (BEAM_BIT + 1)
                out_ref[chunk, place, q % 2] = power.astype(bf16)
        stores[chunk].start()
    for store in stores:
        store.wait()


def filter_power(voltages):
    parts, beams, coarse, upchan, samples = voltages.shape
    chunks = 2
    count = coarse // chunks
    matrix = jnp.asarray(filter_matrix(upchan))
    return pl.pallas_call(
        filter_kernel,
        out_shape=jax.ShapeDtypeStruct((coarse // 2 * beams, 2, upchan, samples), bf16),
        in_specs=[pl.BlockSpec(memory_space=pl.ANY), pl.BlockSpec(memory_space=pl.ANY)],
        out_specs=pl.BlockSpec(memory_space=pl.ANY),
        scratch_shapes=[
            pltpu.VMEM(matrix.shape, bf16),
            pltpu.VMEM((chunks, parts, beams, count, upchan, samples), bf16),
            pltpu.VMEM((chunks, count // 2 * beams, 2, upchan, samples), bf16),
            pltpu.SemaphoreType.DMA((chunks + 1,)),
            pltpu.SemaphoreType.DMA((chunks,)),
        ],
        name="filter_power",
    )(matrix, voltages)


def split_of(x):
    high = x.astype(bf16)
    return jnp.concatenate([high, (x - high.astype(f32)).astype(bf16)], axis=0)


def eye_mask(size):
    row = lax.broadcasted_iota(jnp.int32, (size, size), 0)
    return row == lax.broadcasted_iota(jnp.int32, (size, size), 1)


def columns_of(table):
    eye = jnp.where(eye_mask(table.shape[1]), 1.0, 0.0).astype(bf16)
    columns = lax.dot_general(eye, table.astype(bf16), (((1,), (1,)), ((), ())), preferred_element_type=f32)
    return columns.astype(jnp.int32)


def take_rows(split, weight, source):
    trials = weight.shape[1]
    lane = lax.broadcasted_iota(jnp.int32, (trials, trials), 1)
    picked = jnp.where(lane == source, weight, 0.0).astype(bf16)
    return jnp.dot(jnp.concatenate([picked, picked], axis=1), split, preferred_element_type=f32)


def delay_rows(x, delay):
    trials, samples = x.shape
    half = samples // 2
    lane = lax.broadcasted_iota(jnp.int32, (trials, half), 1)
    index = (lane - delay) & (half - 1)
    inside = lane >= delay
    first = jnp.take_along_axis(x[:, :half], index, axis=1)
    second = jnp.take_along_axis(x[:, half:], index, axis=1)
    return jnp.concatenate([jnp.where(inside, first, 0.0), jnp.where(inside, second, first)], axis=1)


def table_row(level):
    return 3 * (len(KEEPS) - 1 - level)


def table_rows(level):
    return -(-(3 * (len(KEEPS) - level) + 2) // 8) * 8


def merge_unit(split_ref, weight_ref, table, level):
    columns = columns_of(table)
    row = table_row(level)
    lower = take_rows(split_ref[0], weight_ref[0], columns[:, row : row + 1])
    upper = take_rows(split_ref[1], weight_ref[1], columns[:, row + 1 : row + 2])
    return lower + delay_rows(upper, columns[:, row + 2 : row + 3])


def scale_of(code):
    return jnp.exp2(code * (1.0 / 256.0)).astype(bf16).astype(f32)


def put_message(out_ref, x, table):
    trials = x.shape[0]
    rows = out_ref.shape[0] - trials
    peak = jnp.maximum(jnp.max(x, axis=1, keepdims=True), 1e-30)
    code = jnp.floor(jnp.log2(peak) * 256.0) + 3.0
    out_ref[:trials] = ((x * (65536.0 / scale_of(code)) + 0.5).astype(jnp.int32) - 32768).astype(jnp.int16)
    code_row = jnp.sum(jnp.where(eye_mask(trials), code, 0.0), axis=0, keepdims=True).astype(jnp.int32)
    table = table[:rows].astype(jnp.int32)
    row = lax.broadcasted_iota(jnp.int32, table.shape, 0)
    filled = jnp.where(row == rows - 2, code_row >> 8, jnp.where(row == rows - 1, code_row & 255, table))
    out_ref[trials:] = filled.astype(jnp.int16)


def take_message(in_ref, trials):
    table = in_ref[trials:].astype(jnp.int32).astype(f32)
    rows = table.shape[0]
    weight = scale_of(table[rows - 2 : rows - 1] * 256.0 + table[rows - 1 :]) * (1.0 / 65536.0)
    x = in_ref[:trials].astype(jnp.int32) + 32768
    split = jnp.concatenate([(x & 0xFF00).astype(f32).astype(bf16), (x & 0xFF).astype(f32).astype(bf16)], axis=0)
    return split, weight, table


def dedisperse_kernel(arrived_ref, tables_ref, sent_ref, split_ref, weight_ref, table_ref, stack_ref):
    sources, _, upchan, samples = arrived_ref.shape
    trials = weight_ref.shape[2]
    weight_ref[...] = jnp.ones(weight_ref.shape, f32)
    channels = sources * upchan
    for unit in range(2):
        x = arrived_ref[:, unit].reshape(channels, samples).astype(f32)
        for inner in range(INNER):
            moved = x if inner == 0 else shifted(x, inner)
            stack_ref[inner * channels : (inner + 1) * channels] = moved.astype(bf16)
        delays = tables_ref[unit, :trials]
        total = jnp.zeros((trials, samples), f32)
        for outer in reversed(range(SHIFTS // INNER)):
            onehot = jnp.concatenate(
                [
                    jnp.where(delays == jnp.asarray(outer * INNER + inner, bf16), jnp.asarray(1, bf16), jnp.asarray(0, bf16))
                    for inner in range(INNER)
                ],
                axis=1,
            )
            if outer != SHIFTS // INNER - 1:
                total = shifted(total, INNER)
            total = total + jnp.dot(onehot, stack_ref[...], preferred_element_type=f32)
        split_ref[unit] = split_of(total)
        packed = tables_ref[unit, trials:].astype(f32)
        table_ref[unit] = jnp.concatenate([packed[:, :samples], packed[:, samples:]], axis=0)
    put_sent(0, split_ref, weight_ref, table_ref, sent_ref)


def put_sent(level, split_ref, weight_ref, table_ref, sent_ref):
    table = table_ref[1 - KEEPS[level](here())]
    put_message(sent_ref, merge_unit(split_ref, weight_ref, table, level), table)


def kept_kernel(level, split_in_ref, weight_in_ref, table_in_ref, split_ref, table_ref):
    table = table_in_ref[KEEPS[level](here())]
    split_ref[...] = split_of(merge_unit(split_in_ref, weight_in_ref, table, level))
    table_ref[...] = table[: table_ref.shape[0]]


def load_units(own, kept_split_ref, kept_table_ref, received_ref, split_ref, weight_ref, table_ref):
    split_ref[own] = kept_split_ref[...]
    weight_ref[own] = jnp.ones(weight_ref.shape[1:], f32)
    table_ref[own] = kept_table_ref[...]
    split, weight, table = take_message(received_ref, weight_ref.shape[2])
    split_ref[1 - own] = split
    weight_ref[1 - own] = weight
    table_ref[1 - own] = table


def sent_kernel(level, kept_split_ref, kept_table_ref, received_ref, sent_ref, split_ref, weight_ref, table_ref):
    own = bit(here(), level)
    load_units(own, kept_split_ref, kept_table_ref, received_ref, split_ref, weight_ref, table_ref)
    put_sent(level, split_ref, weight_ref, table_ref, sent_ref)


def kept_sent_kernel(level, split_in_ref, weight_in_ref, table_in_ref, message_ref, split_ref):
    table = table_in_ref[KEEPS[level](here())]
    merged = merge_unit(split_in_ref, weight_in_ref, table, level)
    split_ref[...] = split_of(merged)
    put_message(message_ref, merged, table)


def half_kernel(
    level, kept_split_ref, near_ref, across_ref, split_ref, table_ref, across_split_ref, across_weight_ref, splits, weights
):
    own = bit(here(), level)
    splits[own] = kept_split_ref[...]
    weights[own] = jnp.ones(weights.shape[1:], f32)
    split, weight, table = take_message(near_ref, weights.shape[2])
    splits[1 - own] = split
    weights[1 - own] = weight
    split_ref[...] = split_of(merge_unit(splits, weights, table, level))
    table_ref[...] = table
    split, weight, _ = take_message(across_ref, weights.shape[2])
    across_split_ref[...] = split
    across_weight_ref[...] = weight


def quad_kernel(
    level,
    half_split_ref,
    half_table_ref,
    across_split_ref,
    across_weight_ref,
    far_ref,
    sent_ref,
    split_ref,
    weight_ref,
    table_ref,
    splits,
    weights,
):
    own, other = bit(here(), level), bit(here(), level + 1)
    weight_ref[...] = jnp.ones(weight_ref.shape, f32)
    split_ref[other] = half_split_ref[...]
    table_ref[other] = half_table_ref[...]
    splits[own] = across_split_ref[...]
    weights[own] = across_weight_ref[...]
    split, weight, table = take_message(far_ref, weights.shape[2])
    splits[1 - own] = split
    weights[1 - own] = weight
    table_ref[1 - other] = table
    split_ref[1 - other] = split_of(merge_unit(splits, weights, table, level))
    put_sent(level + 1, split_ref, weight_ref, table_ref, sent_ref)


def plus_lagged(x, width):
    if width % 8 == 0:
        return jnp.concatenate([x[:width], x[width:] + x[:-width]], axis=0)
    rolled = pltpu.roll(x, width, 0)
    head = rolled[:8]
    row = lax.broadcasted_iota(jnp.int32, head.shape, 0)
    return x + jnp.concatenate([jnp.where(row >= width, head, 0.0), rolled[8:]], axis=0)


def unit_peaks(merged):
    series = merged.T
    samples = series.shape[0]
    mean = jnp.sum(series, axis=0, keepdims=True) * (1.0 / samples)
    centred = series - mean
    variance = jnp.sum(centred * centred, axis=0, keepdims=True) * (1.0 / samples)
    boxcar = centred * lax.rsqrt(variance + epsilon)
    peaks = [jnp.max(boxcar, axis=0, keepdims=True)]
    width = 1
    for _ in range(1, WIDTHS):
        boxcar = plus_lagged(boxcar, width)
        width *= 2
        peaks.append(jnp.max(boxcar, axis=0, keepdims=True) * (1.0 / math.sqrt(width)))
    return jnp.concatenate(peaks, axis=0)


def sent_peaks_kernel(level, kept_split_ref, kept_table_ref, received_ref, peaks_ref, split_ref, weight_ref, table_ref):
    own = bit(here(), level)
    load_units(own, kept_split_ref, kept_table_ref, received_ref, split_ref, weight_ref, table_ref)
    peaks_ref[...] = unit_peaks(merge_unit(split_ref, weight_ref, table_ref[1 - KEEPS[level](here())], level))


def kept_peaks_kernel(level, split_ref, weight_ref, table_ref, peaks_ref):
    peaks_ref[...] = unit_peaks(merge_unit(split_ref, weight_ref, table_ref[KEEPS[level](here())], level))


def join_kernel(kept_ref, received_ref, out_ref):
    beam = bit(here(), BEAM_BIT)
    out_ref[beam] = kept_ref[...]
    out_ref[1 - beam] = received_ref[...]


VMEM = pl.BlockSpec(memory_space=pltpu.VMEM)


def call(kernel, outs, operands, scratch=(), mebibytes=8):
    return pl.pallas_call(
        kernel,
        out_shape=tuple(jax.ShapeDtypeStruct(shape, dtype) for shape, dtype in outs),
        in_specs=[VMEM] * len(operands),
        out_specs=tuple(VMEM for _ in outs),
        scratch_shapes=list(scratch),
        compiler_params=pltpu.CompilerParams(vmem_limit_bytes=mebibytes << 20),
    )(*operands)


def move(x, target):
    pairs = [(i, target(i)) for i in range(lax.axis_size("freq"))]
    return x if all(i == j for i, j in pairs) else lax.ppermute(x, "freq", pairs)


def swap(x, mask):
    return move(x, lambda i: i ^ mask)


def gather_units(x):
    def target(flip):
        def device(g):
            low = g >> 1 & (1 << BEAM_BIT) - 1
            return low | (bit(g, 0) ^ flip) << BEAM_BIT | g >> (BEAM_BIT + 1) << (BEAM_BIT + 1)

        return device

    return move(x, target(0)), move(x, target(1))


def local(voltages, sub_delays, merge_tables):
    freq_count = lax.axis_size("freq")
    levels = freq_count.bit_length() - 1
    trials, channels = sub_delays.shape
    samples = voltages.shape[4]
    power = filter_power(voltages)
    arrived = lax.all_to_all(power, "freq", split_axis=0, concat_axis=0, tiled=True)

    rows = table_rows(0) // 16 * 16
    table = jnp.pad(merge_tables[::-1].reshape(3 * levels, trials), ((0, rows - 3 * levels), (0, 0)))
    table = table.reshape(2, rows // 2, trials).transpose(1, 0, 2).reshape(rows // 2, 2 * trials)
    first, second = gather_units(jnp.concatenate([sub_delays, table], axis=0).astype(bf16))
    swapped = bit(here(), BEAM_BIT) == 1
    tables = jnp.stack([jnp.where(swapped, second, first), jnp.where(swapped, first, second)])

    def message(level):
        return (trials + table_rows(level), samples), jnp.int16

    def both_units(rows):
        return ((2, 2 * trials, samples), bf16), ((2, 1, trials), f32), ((2, rows, samples), f32)

    stack = pltpu.VMEM((INNER * channels, samples), bf16)
    sent, *both = call(dedisperse_kernel, (message(1), *both_units(rows)), (arrived, tables), [stack], 24)
    pair = ((2 * trials, samples), bf16)
    table = ((table_rows(1), samples), f32)
    scratch = [pltpu.VMEM((2, 2 * trials, samples), bf16), pltpu.VMEM((2, 1, trials), f32)]
    near = swap(sent, PARTNERS[0])
    across = swap(sent, PARTNERS[0] ^ PARTNERS[1])
    same, kept = call(functools.partial(kept_sent_kernel, 0), (message(1), pair), tuple(both))
    far = swap(same, PARTNERS[1])
    outs = (pair, table, pair, ((1, trials), f32))
    half = call(functools.partial(half_kernel, 1), outs, (kept, near, across), scratch)
    outs = (message(3), *both_units(table_rows(1)))
    sent, *both = call(functools.partial(quad_kernel, 1), outs, (*half, far), scratch)
    for level in range(3, levels):
        rows = table_rows(level)
        received = swap(sent, PARTNERS[level - 1])
        units = pair, ((rows, samples), f32)
        kept = call(functools.partial(kept_kernel, level - 1), units, tuple(both))
        last = level == levels - 1
        kernel, _ = (sent_peaks_kernel, "sent_peaks") if last else (sent_kernel, "sent")
        out = ((WIDTHS, trials), f32) if last else message(level + 1)
        sent, *both = call(functools.partial(kernel, level), (out, *both_units(rows)), (*kept, received))
    received = swap(sent, 1 << BEAM_BIT)
    kept = call(functools.partial(kept_peaks_kernel, levels - 1), (out,), tuple(both))
    peaks = call(join_kernel, (((2, WIDTHS, trials), f32),), (*kept, received))[0]
    return move(peaks, home)


def solution(mesh):
    return jax.shard_map(
        local,
        mesh=mesh,
        in_specs=(P(None, "beam", "freq", None, None), P("freq", None), P(None, None, "freq")),
        out_specs=P("beam", None, "freq"),
        check_vma=False,
    )
```
